32 devices in a mesh: section: 4 (over z), node: 4 (over x, core), local: 2 (over y).
Axes of the slice: x: 2, y: 2, z: 4, core: 2. Of those that a mesh axis runs over, the one named last changes fastest.
Arguments:
- section_inputs: bfloat16 [4, 8, 4, 196, 512], P('section', ('node', 'local')), may hold values from -6 to 6
- grad_in: bfloat16 [4, 8, 196, 512], P('section', ('node', 'local')), may hold values from -6 to 6
- loss_grad: bfloat16 [8, 3, 196, 512], P(('node', 'local')), may hold values from -6 to 6
- w_reduce: bfloat16 [4, 512, 256], P('section'), may hold values from -0.25 to 0.25
- w_spatial: bfloat16 [4, 2304, 256], P('section'), may hold values from -0.125 to 0.125
- w_expand: bfloat16 [4, 256, 512], P('section'), may hold values from -0.375 to 0.375
- err_reduce: bfloat16 [4, 8, 512, 256], P('section', ('node', 'local')), may hold values from -360 to 360
- err_spatial: bfloat16 [4, 8, 2304, 256], P('section', ('node', 'local')), may hold values from -360 to 360
- err_expand: bfloat16 [4, 8, 256, 512], P('section', ('node', 'local')), may hold values from -360 to 360
- prior_reduce: float32 [4, 32, 256], P('section'), may hold values from -6 to 6
- prior_spatial: float32 [4, 32, 256], P('section'), may hold values from -6 to 6
- prior_expand: float32 [4, 32, 512], P('section'), may hold values from -6 to 6
Outputs:
- leaving: bfloat16 [4, 8, 196, 512], P('section', ('node', 'local'))
- basis_reduce: float32 [4, 32, 512], P('section', None, ('node', 'local'))
- basis_spatial: float32 [4, 32, 2304], P('section', None, ('node', 'local'))
- basis_expand: float32 [4, 32, 256], P('section', None, ('node', 'local'))
- right_reduce: float32 [4, 32, 256], P('section', None, ('node', 'local'))
- right_spatial: float32 [4, 32, 256], P('section', None, ('node', 'local'))
- right_expand: float32 [4, 32, 512], P('section', None, ('node', 'local'))
The draws below stay inside these ranges and needn't reach their ends.
All inputs are finite; a program needn't handle non-finite values.
Results may differ from the reference program's by a relative error of at most 0.0095.
Values may be sent and summed in bfloat16 or wider, within the bound.
No kernel may reach another device: no remote copies, remote signals or barrier semaphores. Data moves between devices by JAX's collectives and lax.ppermute only.
A program may use at most 128 MiB of HBM per device.

```python
import functools
import math
import jax
import jax.numpy as jnp
from jax import lax

OUT = 512
MID = 256
SIDE = 14
RANK = 32
TICKS = 4
SECTIONS = 4
REPL = 8


def scaled_error(key, salt, row_count, col_count):
    subkeys = jax.random.split(jax.random.fold_in(key, salt), 4)
    full_shape = (SECTIONS, REPL, row_count, col_count)
    rising = 1.0 + 2.0 * jnp.arange(row_count, dtype=jnp.float32) / max(row_count - 1, 1)
    row_scale = jnp.exp(jax.random.uniform(subkeys[0], (SECTIONS, REPL, row_count, 1), jnp.float32) * math.log(10.0))
    random_part = jnp.clip(jax.random.normal(subkeys[3], full_shape, jnp.float32), -4.0, 4.0)
    col_scale = jnp.exp(jax.random.uniform(subkeys[1], (SECTIONS, REPL, 1, col_count), jnp.float32) * math.log(10.0))
    return 0.3 * random_part * row_scale * rising[:, None] * col_scale


def draw_err_reduce(key, part):
    return scaled_error(key, 11, OUT, MID).astype(jnp.bfloat16)


def draw_err_spatial(key, part):
    return scaled_error(key, 12, 9 * MID, MID).astype(jnp.bfloat16)


def draw_err_expand(key, part):
    return scaled_error(key, 13, MID, OUT).astype(jnp.bfloat16)


def shard_levels(stream_key, dims, cuts, low, top_value):
    def one(axis_at, blocks):
        draws = jax.random.uniform(jax.random.fold_in(jax.random.fold_in(stream_key, 6), axis_at), (blocks,), jnp.float32, low / len(cuts), top_value / len(cuts))
        return jnp.repeat(jnp.exp(draws), dims[axis_at] // blocks).reshape((-1,) + (1,) * (len(dims) - axis_at - 1))

    factor_of = one(*cuts[0])
    for cut in cuts[1:]:
        factor_of = factor_of * one(*cut)
    return factor_of


def centred(stream_key, dims, deviation, bound, shards=(), kind=jnp.bfloat16):
    loudness = shard_levels(stream_key, dims, shards, -0.22, 0.18) if shards else 1.0
    values = jax.random.normal(stream_key, dims, jnp.float32) * deviation * loudness
    return jnp.minimum(jnp.maximum(values, -bound), bound).astype(kind)


def setup_inputs(seed: int = 0) -> dict:
    key_of = jax.random.split(jax.random.key(seed), 13)
    section_inputs = centred(key_of[0], (SECTIONS, REPL, TICKS, SIDE * SIDE, OUT), 1.0, 6.0, ((0, 4), (1, 8)))
    grad_in = centred(key_of[1], (SECTIONS, REPL, SIDE * SIDE, OUT), 1.0, 6.0, ((0, 4), (1, 8)))
    loss_grad = centred(key_of[2], (REPL, TICKS - 1, SIDE * SIDE, OUT), 1.0, 6.0, ((0, 8),))
    w_reduce = centred(key_of[3], (SECTIONS, OUT, MID), OUT ** -0.5, 0.25, ((0, 4),))
    w_spatial = centred(key_of[4], (SECTIONS, 9 * MID, MID), (9 * MID) ** -0.5, 0.125, ((0, 4),))
    w_expand = centred(key_of[5], (SECTIONS, MID, OUT), MID ** -0.5, 0.375, ((0, 4),))
    err_reduce = draw_err_reduce(jax.random.fold_in(key_of[12], 71), 0)
    err_spatial = draw_err_spatial(jax.random.fold_in(key_of[12], 71), 0)
    err_expand = draw_err_expand(jax.random.fold_in(key_of[12], 71), 0)
    prior_reduce = centred(key_of[9], (SECTIONS, RANK, MID), 1.0, 6.0, ((0, 4),), jnp.float32)
    prior_spatial = centred(key_of[10], (SECTIONS, RANK, MID), 1.0, 6.0, ((0, 4),), jnp.float32)
    prior_expand = centred(key_of[11], (SECTIONS, RANK, OUT), 1.0, 6.0, ((0, 4),), jnp.float32)
    return dict(section_inputs=section_inputs, grad_in=grad_in, loss_grad=loss_grad, w_reduce=w_reduce, w_spatial=w_spatial, w_expand=w_expand, err_reduce=err_reduce, err_spatial=err_spatial, err_expand=err_expand, prior_reduce=prior_reduce, prior_spatial=prior_spatial, prior_expand=prior_expand)


precise = lax.Precision.HIGHEST

def silu_slope(values):
    logistic = jax.nn.sigmoid(values)
    return logistic * (1.0 + values * (1.0 - logistic))

def expand_taps(hidden, image_side):
    channels = hidden.shape[-1]
    padded = jnp.pad(hidden.reshape(image_side, image_side, channels), ((1, 1), (1, 1), (0, 0)))
    pieces = [padded[row_off:row_off + image_side, col_off:col_off + image_side, :] for row_off in range(3) for col_off in range(3)]
    return jnp.concatenate(pieces, axis=-1).reshape(image_side * image_side, 9 * channels)

def fold_taps(columns, image_side):
    channels = columns.shape[-1] // 9
    blocks = columns.reshape(image_side, image_side, 9, channels)
    running = jnp.zeros((image_side + 2, image_side + 2, channels), jnp.float32)
    for row_off in range(3):
        for col_off in range(3):
            placed = jnp.pad(blocks[:, :, 3 * row_off + col_off, :], ((row_off, 2 - row_off), (col_off, 2 - col_off), (0, 0)))
            running = running + placed
    return running[1:image_side + 1, 1:image_side + 1, :].reshape(image_side * image_side, channels)

def block_backward(inputs, upstream, reduce_weight, spatial_weight, expand_weight, image_side):
    pre_reduce = jnp.dot(inputs.astype(jnp.float32), reduce_weight.astype(jnp.float32), preferred_element_type=jnp.float32)
    hidden_one = jax.nn.silu(pre_reduce).astype(jnp.bfloat16)
    columns = expand_taps(hidden_one, image_side)
    pre_spatial = jnp.dot(columns.astype(jnp.float32), spatial_weight.astype(jnp.float32), preferred_element_type=jnp.float32)
    hidden_two = jax.nn.silu(pre_spatial).astype(jnp.bfloat16)
    back_two = jnp.dot(upstream.astype(jnp.float32), expand_weight.T.astype(jnp.float32), preferred_element_type=jnp.float32)
    back_spatial = (back_two * silu_slope(pre_spatial)).astype(jnp.bfloat16)
    back_columns = jnp.dot(back_spatial.astype(jnp.float32), spatial_weight.T.astype(jnp.float32), preferred_element_type=jnp.float32)
    back_one = fold_taps(back_columns, image_side)
    back_reduce = (back_one * silu_slope(pre_reduce)).astype(jnp.bfloat16)
    leaving = (upstream.astype(jnp.float32) + jnp.dot(back_reduce.astype(jnp.float32), reduce_weight.T.astype(jnp.float32), preferred_element_type=jnp.float32)).astype(jnp.bfloat16)
    gradients = (jnp.dot(inputs.T.astype(jnp.float32), back_reduce.astype(jnp.float32), preferred_element_type=jnp.float32), jnp.dot(columns.T.astype(jnp.float32), back_spatial.astype(jnp.float32), preferred_element_type=jnp.float32), jnp.dot(hidden_two.T.astype(jnp.float32), upstream.astype(jnp.float32), preferred_element_type=jnp.float32))
    return (leaving, gradients)

def compress(gradients, errors, prior):
    matrices = gradients + errors.astype(jnp.float32)
    row_count = matrices.shape[1]
    factor = jnp.einsum('kc,rnc->kn', prior, matrices, precision=precise)
    gram_value = jnp.dot(factor, factor.T, precision=precise)
    triangle = jnp.linalg.cholesky(gram_value)
    orthonormal = lax.linalg.triangular_solve(triangle, factor, left_side=True, lower=True)
    scaled_basis = math.sqrt(row_count) * orthonormal
    loading = jnp.einsum('kn,rnc->kc', orthonormal, matrices, precision=precise) / (REPL * math.sqrt(row_count))
    return (scaled_basis, loading)

def reference(section_inputs, grad_in, loss_grad, w_reduce, w_spatial, w_expand, err_reduce, err_spatial, err_expand, prior_reduce, prior_spatial, prior_expand):
    run_block = jax.vmap(functools.partial(block_backward, image_side=SIDE), in_axes=(0, 0, None, None, None))
    last_flags = jnp.arange(SECTIONS) == SECTIONS - 1

    def one_section(carry_next, section_slice):
        inputs, first_grad, reduce_weight, spatial_weight, expand_weight, error_reduce, error_spatial, error_expand, old_reduce, old_spatial, old_expand, last_section = section_slice
        upstream = first_grad
        totals = (jnp.zeros((REPL, OUT, MID), jnp.float32), jnp.zeros((REPL, 9 * MID, MID), jnp.float32), jnp.zeros((REPL, MID, OUT), jnp.float32))
        handed = []
        for tick_index in range(TICKS):
            if tick_index > 0:
                upstream = jnp.where(last_section, loss_grad[:, tick_index - 1], carry_next[:, tick_index - 1])
            leaving, gradients = run_block(inputs[:, tick_index], upstream, reduce_weight, spatial_weight, expand_weight)
            handed.append(leaving)
            totals = tuple((totals[member] + gradients[member] for member in range(3)))
        basis_one, loading_one = compress(totals[0], error_reduce, old_reduce)
        basis_two, loading_two = compress(totals[1], error_spatial, old_spatial)
        basis_three, loading_three = compress(totals[2], error_expand, old_expand)
        return (jnp.stack(handed, axis=1), (handed[-1], basis_one, basis_two, basis_three, loading_one, loading_two, loading_three))
    initial = jnp.zeros((REPL, TICKS, SIDE * SIDE, OUT), jnp.bfloat16)
    section_data = (section_inputs, grad_in, w_reduce, w_spatial, w_expand, err_reduce, err_spatial, err_expand, prior_reduce, prior_spatial, prior_expand, last_flags)
    final_carry, stacked = lax.scan(one_section, initial, section_data, reverse=True)
    return (stacked[0], stacked[1], stacked[2], stacked[3], stacked[4], stacked[5], stacked[6])
```

```python
import functools
import math

import jax
import jax.numpy as jnp
from jax import lax
from jax.experimental import pallas as pl
from jax.experimental.pallas import tpu as pltpu
from jax.sharding import PartitionSpec as P

F32 = jnp.float32
BF16 = jnp.bfloat16
PAD = 16
REPLICA_AXES = ("node", "local")
precise = lax.Precision.HIGHEST

NN = (((1,), (0,)), ((), ()))
NT = (((1,), (1,)), ((), ()))
TN = (((0,), (0,)), ((), ()))


def mm(left, right, dims=NN, accuracy=None):
    return lax.dot_general(left, right, dims, precision=accuracy, preferred_element_type=F32)


def whole(shape):
    return pl.BlockSpec(shape, lambda i: (0,) * len(shape))


def picked(shape, index):
    return pl.BlockSpec((None,) + shape, lambda i: (index,) + (0,) * len(shape))


def call(body, name, operands, specs, outs, scratch=()):
    return pl.pallas_call(
        body,
        name=name,
        grid=(1,),
        in_specs=specs,
        out_specs=[whole(shape) for shape, _ in outs],
        out_shape=[jax.ShapeDtypeStruct(shape, kind) for shape, kind in outs],
        scratch_shapes=list(scratch),
    )(*operands)


def split(values):
    high = values.astype(BF16)
    low = (values - high.astype(F32)).astype(BF16)
    return jnp.concatenate([high, low], axis=0)


def joined(values):
    rank = values.shape[0] // 2
    return values[:rank] + values[rank:]


def low_rank(prior, grads, inputs):
    inner = joined(mm(split(prior), grads, NT))
    return joined(mm(split(inner), inputs))


def spread_taps(values, padded, columns, side, reverse):
    pixels, channels = values.shape
    column = lax.rem(lax.broadcasted_iota(jnp.int32, (pixels, 1), 0), side)
    zeros = jnp.zeros((PAD, channels), F32)
    for variant in range(3):
        padded[variant, 0:PAD] = zeros
        padded[variant, PAD + pixels : PAD + pixels + PAD] = zeros
    padded[0, PAD : PAD + pixels] = jnp.where(column != side - 1, values, 0.0)
    padded[1, PAD : PAD + pixels] = values
    padded[2, PAD : PAD + pixels] = jnp.where(column != 0, values, 0.0)
    for tap in range(9):
        source = 8 - tap if reverse else tap
        start = PAD + (source // 3 - 1) * side + source % 3 - 1
        columns[:, tap * channels : (tap + 1) * channels] = padded[
            source % 3, start : start + pixels
        ].astype(BF16)


def forward(inputs, w_reduce, w_spatial, padded, columns, hidden, slope_one, slope_two, side):
    pre = mm(inputs[...], w_reduce[...])
    logistic = jax.nn.sigmoid(pre)
    slope_one[...] = logistic * (1.0 + pre * (1.0 - logistic))
    spread_taps(pre * logistic, padded, columns, side, False)
    pre = mm(columns[...], w_spatial[...])
    logistic = jax.nn.sigmoid(pre)
    slope_two[...] = logistic * (1.0 + pre * (1.0 - logistic))
    hidden[...] = (pre * logistic).astype(BF16)


def backward(up, w_reduce, w_spatial, w_expand, slope_one, slope_two, padded, taps, side):
    channels = slope_one.shape[1]
    grad = mm(up, w_expand[...], NT) * slope_two[...]
    spread_taps(grad, padded, taps, side, True)
    back = None
    for tap in range(9):
        block = slice(tap * channels, (tap + 1) * channels)
        term = mm(taps[:, block], w_spatial[block, :], NT)
        back = term if back is None else back + term
    grad_two = grad.astype(BF16)
    grad_one = (back * slope_one[...]).astype(BF16)
    leaving = (up.astype(F32) + mm(grad_one, w_reduce[...], NT)).astype(BF16)
    return grad_two, grad_one, leaving


def first_body(side, x, up, wr, ws, we, cols, hid, gb, ga, dx, padded, taps, s1, s2):
    forward(x, wr, ws, padded, cols, hid, s1, s2, side)
    gb[...], ga[...], dx[...] = backward(up[...], wr, ws, we, s1, s2, padded, taps, side)


def ahead_body(side, count, x, wr, ws, *refs):
    padded = refs[-1]
    for step in range(count):
        cols, hid, s1, s2 = refs[4 * step : 4 * step + 4]
        forward(x.at[step + 1], wr, ws, padded, cols, hid, s1, s2, side)


def chosen(arrived, loss):
    last = lax.axis_index("section") == lax.axis_size("section") - 1
    return jnp.where(last, loss[...], arrived[...])


def middle_body(side, arrived, loss, wr, ws, we, s1, s2, up, gb, ga, dx, padded, taps):
    value = chosen(arrived, loss)
    up[...] = value
    gb[...], ga[...], dx[...] = backward(value, wr, ws, we, s1, s2, padded, taps, side)


def start_body(er, es, ee, pr, ps, pe, pt, etr, ets):
    rows, spatial = er.shape[0], es.shape[0]
    pt[:, 0:rows] = joined(mm(split(pr[...]), er[...], NT))
    pt[:, rows : rows + spatial] = joined(mm(split(ps[...]), es[...], NT))
    pt[:, rows + spatial :] = joined(mm(split(pe[...]), ee[...], NT))
    etr[...] = er[...].astype(F32).T
    ets[...] = es[...].astype(F32).T


def add_factor(pt_in, pt_out, x, cols, hid, up, gb, ga, pr, ps, pe):
    rows, spatial = x.shape[1], cols.shape[1]
    end = rows + spatial
    pt_out[:, 0:rows] = pt_in[:, 0:rows] + low_rank(pr[...], ga, x[...])
    pt_out[:, rows:end] = pt_in[:, rows:end] + low_rank(ps[...], gb, cols[...])
    pt_out[:, end:] = pt_in[:, end:] + low_rank(pe[...], up, hid[...])


def sums_body(count, x, etr, ets, ee, pt, pr, ps, pe, *refs):
    pt_out, mr, ms, me = refs[-4:]
    source = pt
    for step in range(count):
        cols, hid, up, gb, ga = refs[5 * step : 5 * step + 5]
        add_factor(source, pt_out, x.at[step], cols, hid, up[...], gb[...], ga[...], pr, ps, pe)
        source = pt_out
    for step in range(count):
        cols, hid, up, gb, ga = refs[5 * step : 5 * step + 5]
        base_r = etr[...] if step == 0 else mr[...]
        mr[...] = base_r + mm(ga[...], x[step], TN)
        base_s = ets[...] if step == 0 else ms[...]
        ms[...] = base_s + mm(gb[...], cols[...], TN)
        base_e = ee[...].astype(F32) if step == 0 else me[...]
        me[...] = base_e + mm(hid[...], up[...], TN)


def last_body(side, x, arrived, loss, wr, ws, we, cols, hid, s1, s2, pt, pr, ps, pe,
              up, gb, ga, dx, *refs):
    outs, (padded, taps, factor) = refs[:-3], refs[-3:]
    value = chosen(arrived, loss)
    up[...] = value
    gb[...], ga[...], dx[...] = backward(value, wr, ws, we, s1, s2, padded, taps, side)
    if len(outs) == 1:
        add_factor(pt, outs[0], x, cols, hid, value, gb[...], ga[...], pr, ps, pe)
        return
    add_factor(pt, factor, x, cols, hid, value, gb[...], ga[...], pr, ps, pe)
    keep, send = outs
    chips, _, width = keep.shape
    me = lax.axis_index(REPLICA_AXES)
    for chip in range(chips):
        kept = pl.multiple_of((me ^ flips(chip, False)) * width, width)
        keep[chip] = factor[:, pl.ds(kept, width)]
        sent = pl.multiple_of((me ^ flips(chip, True)) * width, width)
        send[chip] = factor[:, pl.ds(sent, width)].astype(BF16)


def finish_body(x, mr, ms, me, cols, hid, up, gb, ga, br, bs, be):
    br[...] = (mr[...] + mm(ga[...], x[...], TN)).astype(BF16)
    bs[...] = (ms[...] + mm(gb[...], cols[...], TN)).astype(BF16)
    be[...] = (me[...] + mm(hid[...], up[...], TN)).astype(BF16)


def flips(chip, other_core):
    local_bits = lax.axis_size("local").bit_length() - 1
    low = chip & (lax.axis_size("local") - 1)
    high = chip >> local_bits
    return low | (int(other_core) << local_bits) | (high << (local_bits + 1))


def swap(values, mask):
    count = lax.axis_size(REPLICA_AXES)
    return lax.ppermute(values, REPLICA_AXES, [(i, i ^ mask) for i in range(count)])


def fold_body(keep, got, own, *sends):
    own[...] = keep[0] + got[0].astype(F32)
    for chip, send in enumerate(sends, 1):
        send[...] = (keep[chip] + got[chip].astype(F32)).astype(BF16)


def total_body(own, *refs):
    total = own[...]
    for ref in refs[:-1]:
        total = total + ref[...].astype(F32)
    refs[-1][...] = total.astype(BF16)


def right_body(chips, *refs):
    mine = refs[:chips]
    other, br, bs, be, pt, keep, send, flat, pieces = refs[chips:]
    me = lax.axis_index(REPLICA_AXES)
    width = flat.shape[1] // (2 * chips)
    for chip in range(chips):
        at = pl.multiple_of((me ^ flips(chip, False)) * width, width)
        flat[:, pl.ds(at, width)] = mine[chip][...].astype(F32)
        at = pl.multiple_of((me ^ flips(chip, True)) * width, width)
        flat[:, pl.ds(at, width)] = other[chip].astype(F32)
    full = flat[...].astype(BF16)
    pt[...] = full
    rows, spatial = br.shape[1], bs.shape[1]
    parts = (
        mm(full[:, :rows], br[...], NT),
        mm(full[:, rows : rows + spatial], bs[...], NT),
        mm(full[:, rows + spatial :], be[...]),
    )
    count = 2 * chips
    for piece in range(count):
        cut = []
        for part in parts:
            wide = part.shape[1] // count
            cut.append(part[:, piece * wide : (piece + 1) * wide])
        pieces[piece] = jnp.concatenate(cut, axis=1)
    for chip in range(chips):
        keep[chip] = pieces[me ^ flips(chip, False)]
        send[chip] = pieces[me ^ flips(chip, True)].astype(BF16)


def inverse_factor(gram):
    rank = gram.shape[0]
    row = lax.broadcasted_iota(jnp.int32, (rank, 2 * rank), 0)
    lane = lax.broadcasted_iota(jnp.int32, (rank, 2 * rank), 1)
    table = jnp.concatenate([gram, jnp.zeros_like(gram)], axis=1)
    table = jnp.where(lane == row + rank, 1.0, table)
    scale = jnp.zeros((rank, 1), F32)
    for step in range(rank):
        column = table[:, step : step + 1]
        pivot = table[step : step + 1, step : step + 1]
        ratio = column / pivot
        scale = jnp.where(row[:, :1] == step, lax.rsqrt(pivot), scale)
        table = jnp.where(row > step, table - ratio * table[step : step + 1, :], table)
    return table[:, rank:] * scale


def basis_body(splits, pt, inverse, *outs):
    me = lax.axis_index(REPLICA_AXES)
    count = lax.axis_size(REPLICA_AXES)
    start = 0
    for member, rows in enumerate(splits):
        full = pt[:, start : start + rows]
        linv = inverse_factor(mm(full, full, NT))
        inverse[member] = linv
        wide = rows // count
        window = min(-(-wide // 128) * 128 + (128 if 128 % wide and wide % 128 else 0), rows)
        first = me * wide
        aligned = pl.multiple_of(first // 128 * 128, 128)
        block = pt[:, pl.ds(start + aligned, window)].astype(F32)
        moved = pltpu.roll(block, lax.rem(window - (first - aligned), window), 1)
        outs[member][...] = math.sqrt(rows) * mm(linv, moved[:, :wide], NN, precise)
        start += rows


def end_body(splits, replicas, inverse, own, a, b, c, *outs):
    total = own[...] + a[...].astype(F32) + b[...].astype(F32) + c[...].astype(F32)
    start = 0
    for member, out in enumerate(outs):
        wide = out.shape[1]
        scale = 1.0 / (replicas * math.sqrt(splits[member]))
        out[...] = scale * mm(inverse[member], total[:, start : start + wide], NN, precise)
        start += wide


def shifted(block):
    count = lax.axis_size("section")
    return lax.ppermute(block, "section", [(i, i - 1) for i in range(1, count)])


def specs_of(operands):
    return [whole(operand.shape) for operand in operands]


def general_tail(pt, matrices, splits):
    replicas = lax.axis_size(REPLICA_AXES)
    me = lax.axis_index(REPLICA_AXES)
    total = lax.psum(pt, REPLICA_AXES)
    bases, rights = [], []
    start = 0
    for member, rows in enumerate(splits):
        part = total[:, start : start + rows]
        start += rows
        triangle = jnp.linalg.cholesky(mm(part, part, NT, precise))
        unit = lax.linalg.triangular_solve(triangle, part, left_side=True, lower=True)
        wide = rows // replicas
        own = lax.dynamic_slice_in_dim(unit, me * wide, wide, 1)
        bases.append(math.sqrt(rows) * own)
        matrix = matrices[member].astype(F32)
        dims = NN if member == 2 else NT
        right = mm(unit, matrix, dims, precise)
        right = lax.psum_scatter(
            right.astype(BF16), REPLICA_AXES, scatter_dimension=1, tiled=True
        ).astype(F32)
        rights.append(right / (replicas * math.sqrt(rows)))
    return bases, rights


def local(
    section_inputs,
    grad_in,
    loss_grad,
    w_reduce,
    w_spatial,
    w_expand,
    err_reduce,
    err_spatial,
    err_expand,
    prior_reduce,
    prior_spatial,
    prior_expand,
):
    x = section_inputs[0, 0]
    loss = loss_grad[0]
    wr, ws, we = w_reduce[0], w_spatial[0], w_expand[0]
    er, es, ee = err_reduce[0, 0], err_spatial[0, 0], err_expand[0, 0]
    pr, ps, pe = prior_reduce[0], prior_spatial[0], prior_expand[0]
    ticks, pixels, out = x.shape
    mid = wr.shape[1]
    taps = ws.shape[0]
    rank = pr.shape[0]
    side = math.isqrt(pixels)
    total = out + taps + mid
    splits = (out, taps, mid)

    image = (pixels, out)
    inner = (pixels, mid)
    wide = (pixels, taps)
    padded = pltpu.VMEM((3, pixels + 2 * PAD, mid), F32)
    tap_space = pltpu.VMEM(wide, BF16)
    saved = [(wide, BF16), (inner, BF16), (inner, F32), (inner, F32)]
    grads = [(inner, BF16), (inner, BF16), (image, BF16)]

    weights = (wr, ws, we)
    up = grad_in[0, 0]
    cols, hid, gb, ga, dx = call(
        functools.partial(first_body, side),
        "first_tick",
        (x, up) + weights,
        [picked(image, 0)] + specs_of((up,) + weights),
        saved[:2] + grads,
        (padded, tap_space, pltpu.VMEM(inner, F32), pltpu.VMEM(inner, F32)),
    )
    done = [(cols, hid, up, gb, ga)]
    arrived = shifted(dx)
    ahead = call(
        functools.partial(ahead_body, side, ticks - 1),
        "forward_ahead",
        (x, wr, ws),
        specs_of((x, wr, ws)),
        saved * (ticks - 1),
        (padded,),
    )
    pt, etr, ets = call(
        start_body,
        "error_terms",
        (er, es, ee, pr, ps, pe),
        specs_of((er, es, ee, pr, ps, pe)),
        [((rank, total), F32), ((mid, out), F32), ((mid, taps), F32)],
    )
    for tick in range(1, ticks - 1):
        cols, hid, s1, s2 = ahead[4 * tick - 4 : 4 * tick]
        operands = weights + (s1, s2)
        up, gb, ga, dx = call(
            functools.partial(middle_body, side),
            "middle_tick",
            (arrived, loss) + operands,
            [whole(image), picked(image, tick - 1)] + specs_of(operands),
            [(image, BF16)] + grads,
            (padded, tap_space),
        )
        done.append((cols, hid, up, gb, ga))
        arrived = shifted(dx)
    flat = tuple(part for group in done for part in group)
    operands = (x, etr, ets, ee, pt, pr, ps, pe) + flat
    pt, mr, ms, me = call(
        functools.partial(sums_body, ticks - 1),
        "running_sums",
        operands,
        specs_of(operands),
        [((rank, total), F32), ((mid, out), F32), ((mid, taps), F32), ((mid, out), F32)],
    )

    replicas = lax.axis_size(REPLICA_AXES)
    piece = total // replicas
    fast = replicas == 8 and lax.axis_size("node") == 4 and piece % 128 == 0
    chips = replicas // 2
    cols, hid, s1, s2 = ahead[4 * ticks - 8 : 4 * ticks - 4]
    operands = weights + (cols, hid, s1, s2, pt, pr, ps, pe)
    parts = (chips, rank, piece)
    extra = [(parts, F32), (parts, BF16)] if fast else [((rank, total), F32)]
    up, gb, ga, leaving, *factor = call(
        functools.partial(last_body, side),
        "last_tick",
        (x, arrived, loss) + operands,
        [picked(image, ticks - 1), whole(image), picked(image, ticks - 2)] + specs_of(operands),
        [(image, BF16)] + grads + extra,
        (padded, tap_space, pltpu.VMEM((rank, total), F32)),
    )
    operands = (mr, ms, me, cols, hid, up, gb, ga)
    matrices = call(
        finish_body,
        "final_sums",
        (x,) + operands,
        [picked(image, ticks - 1)] + specs_of(operands),
        [((mid, out), BF16), ((mid, taps), BF16), ((mid, out), BF16)],
    )
    if not fast:
        bases, rights = general_tail(factor[0], matrices, splits)
        return tuple(value[None] for value in [leaving[None], *bases, *rights])

    def scattered(keep, send, name):
        got = swap(send, flips(0, True))
        own, *sends = call(
            fold_body,
            name,
            (keep, got),
            specs_of((keep, got)),
            [(keep.shape[1:], F32)] + [(keep.shape[1:], BF16)] * (chips - 1),
        )
        return own, [swap(value, flips(chip, False)) for chip, value in enumerate(sends, 1)]

    own, others = scattered(*factor, "fold_factor")
    (own,) = call(
        total_body,
        "total_factor",
        (own, *others),
        specs_of((own, *others)),
        [((rank, piece), BF16)],
    )
    mine = [own] + [swap(own, flips(chip, False)) for chip in range(1, chips)]
    other = swap(jnp.stack(mine), flips(0, True))
    part = (mid + mid + out) // replicas
    operands = (*mine, other, *matrices)
    pt, keep, send = call(
        functools.partial(right_body, chips),
        "right_products",
        operands,
        specs_of(operands),
        [((rank, total), BF16), ((chips, rank, part), F32), ((chips, rank, part), BF16)],
        (pltpu.VMEM((rank, total), F32), pltpu.VMEM((replicas, rank, part), F32)),
    )
    own, others = scattered(keep, send, "fold_right")
    inverse, *bases = call(
        functools.partial(basis_body, splits),
        "basis",
        (pt,),
        specs_of((pt,)),
        [((3, rank, rank), F32)] + [((rank, rows // replicas), F32) for rows in splits],
    )
    operands = (inverse, own, *others)
    rights = call(
        functools.partial(end_body, splits, replicas),
        "right_factors",
        operands,
        specs_of(operands),
        [((rank, columns // replicas), F32) for columns in (mid, mid, out)],
    )
    return tuple(value[None] for value in [leaving[None], *bases, *rights])


def solution(mesh):
    replica = P("section", REPLICA_AXES)
    weight = P("section")
    column = P("section", None, REPLICA_AXES)
    return jax.shard_map(
        local,
        mesh=mesh,
        in_specs=(replica, replica, P(REPLICA_AXES)) + (weight,) * 3 + (replica,) * 3 + (weight,) * 3,
        out_specs=(replica,) + (column,) * 6,
        check_vma=False,
    )
```

```python
import functools
import math

import jax
import jax.numpy as jnp
from jax import lax
from jax.experimental import pallas as pl
from jax.experimental.pallas import tpu as pltpu
from jax.sharding import PartitionSpec as P

F32 = jnp.float32
BF16 = jnp.bfloat16
PAD = 16
VMEM_LIMIT = 16 * 1024 * 1024
REPLICA_AXES = ("node", "local")
precise = lax.Precision.HIGHEST

NN = (((1,), (0,)), ((), ()))
NT = (((1,), (1,)), ((), ()))
TN = (((0,), (0,)), ((), ()))


def mm(left, right, dims=NN, accuracy=None):
    return lax.dot_general(left, right, dims, precision=accuracy, preferred_element_type=F32)


def call(body, name, operands, outs, scratch=(), results=0):
    kept = len(outs) - results
    return pl.pallas_call(
        body,
        name=name,
        in_specs=[pl.BlockSpec(memory_space=pltpu.VMEM)] * len(operands),
        out_specs=[pl.BlockSpec(memory_space=pltpu.VMEM)] * len(outs),
        out_shape=[pltpu.VMEM(*out) for out in outs[:kept]]
        + [jax.ShapeDtypeStruct(*out) for out in outs[kept:]],
        scratch_shapes=list(scratch),
        compiler_params=pltpu.CompilerParams(vmem_limit_bytes=VMEM_LIMIT),
    )(*[pltpu.with_memory_space_constraint(operand, pltpu.VMEM) for operand in operands])


def split(values):
    high = values.astype(BF16)
    low = (values - high.astype(F32)).astype(BF16)
    return jnp.concatenate([high, low], axis=0)


def joined(values):
    rank = values.shape[0] // 2
    return values[:rank] + values[rank:]


def low_rank(prior, grads, inputs):
    inner = joined(mm(split(prior), grads, NT))
    return joined(mm(split(inner), inputs))


def spread_taps(values, padded, columns, side, reverse):
    pixels, channels = values.shape
    column = lax.rem(lax.broadcasted_iota(jnp.int32, (pixels, 1), 0), side)
    zeros = jnp.zeros((PAD, channels), F32)
    for variant in range(3):
        padded[variant, 0:PAD] = zeros
        padded[variant, PAD + pixels : PAD + pixels + PAD] = zeros
    padded[0, PAD : PAD + pixels] = jnp.where(column != side - 1, values, 0.0)
    padded[1, PAD : PAD + pixels] = values
    padded[2, PAD : PAD + pixels] = jnp.where(column != 0, values, 0.0)
    for tap in range(9):
        source = 8 - tap if reverse else tap
        start = PAD + (source // 3 - 1) * side + source % 3 - 1
        columns[:, tap * channels : (tap + 1) * channels] = padded[
            source % 3, start : start + pixels
        ].astype(BF16)


def forward(inputs, w_reduce, w_spatial, padded, columns, hidden, slope_one, slope_two, side):
    pre = mm(inputs[...], w_reduce[...])
    logistic = jax.nn.sigmoid(pre)
    slope_one[...] = logistic * (1.0 + pre * (1.0 - logistic))
    spread_taps(pre * logistic, padded, columns, side, False)
    pre = mm(columns[...], w_spatial[...])
    logistic = jax.nn.sigmoid(pre)
    slope_two[...] = logistic * (1.0 + pre * (1.0 - logistic))
    hidden[...] = (pre * logistic).astype(BF16)


def backward(up, w_reduce, w_spatial, w_expand, slope_one, slope_two, padded, taps, side):
    channels = slope_one.shape[1]
    grad = mm(up, w_expand[...], NT) * slope_two[...]
    spread_taps(grad, padded, taps, side, True)
    back = None
    for tap in range(9):
        block = slice(tap * channels, (tap + 1) * channels)
        term = mm(taps[:, block], w_spatial[block, :], NT)
        back = term if back is None else back + term
    grad_two = grad.astype(BF16)
    grad_one = (back * slope_one[...]).astype(BF16)
    leaving = (up.astype(F32) + mm(grad_one, w_reduce[...], NT)).astype(BF16)
    return grad_two, grad_one, leaving


def first_body(side, x, up, wr, ws, we, cols, hid, gb, ga, dx, padded, taps, s1, s2):
    forward(x.at[0], wr, ws, padded, cols, hid, s1, s2, side)
    gb[...], ga[...], dx[...] = backward(up[...], wr, ws, we, s1, s2, padded, taps, side)


def ahead_body(side, count, x, wr, ws, *refs):
    padded = refs[-1]
    for step in range(count):
        cols, hid, s1, s2 = refs[4 * step : 4 * step + 4]
        forward(x.at[step + 1], wr, ws, padded, cols, hid, s1, s2, side)


def chosen(arrived, loss, tick):
    last = lax.axis_index("section") == lax.axis_size("section") - 1
    return jnp.where(last, loss[tick - 1], arrived[...])


def middle_body(side, tick, arrived, loss, wr, ws, we, s1, s2, up, gb, ga, dx, padded, taps):
    value = chosen(arrived, loss, tick)
    up[...] = value
    gb[...], ga[...], dx[...] = backward(value, wr, ws, we, s1, s2, padded, taps, side)


def start_body(er, es, ee, pr, ps, pe, pt, etr, ets):
    rows, spatial = er.shape[0], es.shape[0]
    pt[:, 0:rows] = joined(mm(split(pr[...]), er[...], NT))
    pt[:, rows : rows + spatial] = joined(mm(split(ps[...]), es[...], NT))
    pt[:, rows + spatial :] = joined(mm(split(pe[...]), ee[...], NT))
    etr[...] = er[...].astype(F32).T
    ets[...] = es[...].astype(F32).T


def add_factor(pt_in, pt_out, x, cols, hid, up, gb, ga, pr, ps, pe):
    rows, spatial = x.shape[1], cols.shape[1]
    end = rows + spatial
    pt_out[:, 0:rows] = pt_in[:, 0:rows] + low_rank(pr[...], ga, x[...])
    pt_out[:, rows:end] = pt_in[:, rows:end] + low_rank(ps[...], gb, cols[...])
    pt_out[:, end:] = pt_in[:, end:] + low_rank(pe[...], up, hid[...])


def sums_body(count, x, etr, ets, ee, pt, pr, ps, pe, *refs):
    pt_out, mr, ms, me = refs[-4:]
    source = pt
    for step in range(count):
        cols, hid, up, gb, ga = refs[5 * step : 5 * step + 5]
        add_factor(source, pt_out, x.at[step], cols, hid, up[...], gb[...], ga[...], pr, ps, pe)
        source = pt_out
    for step in range(count):
        cols, hid, up, gb, ga = refs[5 * step : 5 * step + 5]
        base_r = etr[...] if step == 0 else mr[...]
        mr[...] = base_r + mm(ga[...], x[step], TN)
        base_s = ets[...] if step == 0 else ms[...]
        ms[...] = base_s + mm(gb[...], cols[...], TN)
        base_e = ee[...].astype(F32) if step == 0 else me[...]
        me[...] = base_e + mm(hid[...], up[...], TN)


def last_body(side, tick, x, arrived, loss, wr, ws, we, cols, hid, s1, s2, pt, pr, ps, pe,
              up, gb, ga, dx, *refs):
    outs, (padded, taps, factor) = refs[:-3], refs[-3:]
    value = chosen(arrived, loss, tick)
    up[...] = value
    gb[...], ga[...], dx[...] = backward(value, wr, ws, we, s1, s2, padded, taps, side)
    if len(outs) == 1:
        add_factor(pt, outs[0], x.at[tick], cols, hid, value, gb[...], ga[...], pr, ps, pe)
        return
    add_factor(pt, factor, x.at[tick], cols, hid, value, gb[...], ga[...], pr, ps, pe)
    keep, send = outs
    chips, _, width = keep.shape
    me = lax.axis_index(REPLICA_AXES)
    for chip in range(chips):
        kept = pl.multiple_of((me ^ flips(chip, False)) * width, width)
        keep[chip] = factor[:, pl.ds(kept, width)]
        sent = pl.multiple_of((me ^ flips(chip, True)) * width, width)
        send[chip] = factor[:, pl.ds(sent, width)].astype(BF16)


def finish_body(tick, x, mr, ms, me, cols, hid, up, gb, ga, br, bs, be):
    br[...] = (mr[...] + mm(ga[...], x[tick], TN)).astype(BF16)
    bs[...] = (ms[...] + mm(gb[...], cols[...], TN)).astype(BF16)
    be[...] = (me[...] + mm(hid[...], up[...], TN)).astype(BF16)


def flips(chip, other_core):
    local_bits = lax.axis_size("local").bit_length() - 1
    low = chip & (lax.axis_size("local") - 1)
    high = chip >> local_bits
    return low | (int(other_core) << local_bits) | (high << (local_bits + 1))


def swap(values, mask):
    count = lax.axis_size(REPLICA_AXES)
    return lax.ppermute(values, REPLICA_AXES, [(i, i ^ mask) for i in range(count)])


def fold_body(keep, got, own, *sends):
    own[...] = keep[0] + got[0].astype(F32)
    for chip, send in enumerate(sends, 1):
        send[...] = (keep[chip] + got[chip].astype(F32)).astype(BF16)


def total_body(own, *refs):
    total = own[...]
    for ref in refs[:-1]:
        total = total + ref[...].astype(F32)
    refs[-1][...] = total.astype(BF16)


def right_body(chips, *refs):
    mine = refs[:chips]
    other, br, bs, be, pt, keep, send, flat, pieces = refs[chips:]
    me = lax.axis_index(REPLICA_AXES)
    width = flat.shape[1] // (2 * chips)
    for chip in range(chips):
        at = pl.multiple_of((me ^ flips(chip, False)) * width, width)
        flat[:, pl.ds(at, width)] = mine[chip][...].astype(F32)
        at = pl.multiple_of((me ^ flips(chip, True)) * width, width)
        flat[:, pl.ds(at, width)] = other[chip].astype(F32)
    full = flat[...].astype(BF16)
    pt[...] = full
    rows, spatial = br.shape[1], bs.shape[1]
    parts = (
        mm(full[:, :rows], br[...], NT),
        mm(full[:, rows : rows + spatial], bs[...], NT),
        mm(full[:, rows + spatial :], be[...]),
    )
    count = 2 * chips
    for piece in range(count):
        cut = []
        for part in parts:
            wide = part.shape[1] // count
            cut.append(part[:, piece * wide : (piece + 1) * wide])
        pieces[piece] = jnp.concatenate(cut, axis=1)
    for chip in range(chips):
        keep[chip] = pieces[me ^ flips(chip, False)]
        send[chip] = pieces[me ^ flips(chip, True)].astype(BF16)


def inverse_factor(gram):
    rank = gram.shape[0]
    row = lax.broadcasted_iota(jnp.int32, (rank, 2 * rank), 0)
    lane = lax.broadcasted_iota(jnp.int32, (rank, 2 * rank), 1)
    table = jnp.concatenate([gram, jnp.zeros_like(gram)], axis=1)
    table = jnp.where(lane == row + rank, 1.0, table)
    scale = jnp.zeros((rank, 1), F32)
    for step in range(rank):
        column = table[:, step : step + 1]
        pivot = table[step : step + 1, step : step + 1]
        ratio = column / pivot
        scale = jnp.where(row[:, :1] == step, lax.rsqrt(pivot), scale)
        table = jnp.where(row > step, table - ratio * table[step : step + 1, :], table)
    return table[:, rank:] * scale


def basis_body(splits, pt, inverse, *outs):
    me = lax.axis_index(REPLICA_AXES)
    count = lax.axis_size(REPLICA_AXES)
    start = 0
    for member, rows in enumerate(splits):
        full = pt[:, start : start + rows]
        linv = inverse_factor(mm(full, full, NT))
        inverse[member] = linv
        wide = rows // count
        window = min(-(-wide // 128) * 128 + (128 if 128 % wide and wide % 128 else 0), rows)
        first = me * wide
        aligned = pl.multiple_of(first // 128 * 128, 128)
        block = pt[:, pl.ds(start + aligned, window)].astype(F32)
        moved = pltpu.roll(block, lax.rem(window - (first - aligned), window), 1)
        outs[member][...] = math.sqrt(rows) * mm(linv, moved[:, :wide], NN, precise)
        start += rows


def end_body(splits, replicas, inverse, own, a, b, c, *outs):
    total = own[...] + a[...].astype(F32) + b[...].astype(F32) + c[...].astype(F32)
    start = 0
    for member, out in enumerate(outs):
        wide = out.shape[1]
        scale = 1.0 / (replicas * math.sqrt(splits[member]))
        out[...] = scale * mm(inverse[member], total[:, start : start + wide], NN, precise)
        start += wide


def shifted(block):
    count = lax.axis_size("section")
    return lax.ppermute(block, "section", [(i, i - 1) for i in range(1, count)])


def general_tail(pt, matrices, splits):
    replicas = lax.axis_size(REPLICA_AXES)
    me = lax.axis_index(REPLICA_AXES)
    total = lax.psum(pt, REPLICA_AXES)
    bases, rights = [], []
    start = 0
    for member, rows in enumerate(splits):
        part = total[:, start : start + rows]
        start += rows
        triangle = jnp.linalg.cholesky(mm(part, part, NT, precise))
        unit = lax.linalg.triangular_solve(triangle, part, left_side=True, lower=True)
        wide = rows // replicas
        own = lax.dynamic_slice_in_dim(unit, me * wide, wide, 1)
        bases.append(math.sqrt(rows) * own)
        matrix = matrices[member].astype(F32)
        dims = NN if member == 2 else NT
        right = mm(unit, matrix, dims, precise)
        right = lax.psum_scatter(
            right.astype(BF16), REPLICA_AXES, scatter_dimension=1, tiled=True
        ).astype(F32)
        rights.append(right / (replicas * math.sqrt(rows)))
    return bases, rights


def local(
    section_inputs,
    grad_in,
    loss_grad,
    w_reduce,
    w_spatial,
    w_expand,
    err_reduce,
    err_spatial,
    err_expand,
    prior_reduce,
    prior_spatial,
    prior_expand,
):
    x = section_inputs[0, 0]
    loss = loss_grad[0]
    wr, ws, we = w_reduce[0], w_spatial[0], w_expand[0]
    er, es, ee = err_reduce[0, 0], err_spatial[0, 0], err_expand[0, 0]
    pr, ps, pe = prior_reduce[0], prior_spatial[0], prior_expand[0]
    ticks, pixels, out = x.shape
    mid = wr.shape[1]
    taps = ws.shape[0]
    rank = pr.shape[0]
    side = math.isqrt(pixels)
    total = out + taps + mid
    splits = (out, taps, mid)

    image = (pixels, out)
    inner = (pixels, mid)
    wide = (pixels, taps)
    padded = pltpu.VMEM((3, pixels + 2 * PAD, mid), F32)
    tap_space = pltpu.VMEM(wide, BF16)
    saved = [(wide, BF16), (inner, BF16), (inner, F32), (inner, F32)]
    grads = [(inner, BF16), (inner, BF16), (image, BF16)]

    weights = (wr, ws, we)
    up = grad_in[0, 0]
    cols, hid, gb, ga, dx = call(
        functools.partial(first_body, side),
        "first_tick",
        (x, up) + weights,
        saved[:2] + grads,
        (padded, tap_space, pltpu.VMEM(inner, F32), pltpu.VMEM(inner, F32)),
    )
    done = [(cols, hid, up, gb, ga)]
    arrived = shifted(dx)
    ahead = call(
        functools.partial(ahead_body, side, ticks - 1),
        "forward_ahead",
        (x, wr, ws),
        saved * (ticks - 1),
        (padded,),
    )
    pt, etr, ets = call(
        start_body,
        "error_terms",
        (er, es, ee, pr, ps, pe),
        [((rank, total), F32), ((mid, out), F32), ((mid, taps), F32)],
    )
    for tick in range(1, ticks - 1):
        cols, hid, s1, s2 = ahead[4 * tick - 4 : 4 * tick]
        operands = weights + (s1, s2)
        up, gb, ga, dx = call(
            functools.partial(middle_body, side, tick),
            "middle_tick",
            (arrived, loss) + operands,
            [(image, BF16)] + grads,
            (padded, tap_space),
        )
        done.append((cols, hid, up, gb, ga))
        arrived = shifted(dx)
    flat = tuple(part for group in done for part in group)
    operands = (x, etr, ets, ee, pt, pr, ps, pe) + flat
    pt, mr, ms, me = call(
        functools.partial(sums_body, ticks - 1),
        "running_sums",
        operands,
        [((rank, total), F32), ((mid, out), F32), ((mid, taps), F32), ((mid, out), F32)],
    )

    replicas = lax.axis_size(REPLICA_AXES)
    piece = total // replicas
    fast = replicas == 8 and lax.axis_size("node") == 4 and piece % 128 == 0
    chips = replicas // 2
    cols, hid, s1, s2 = ahead[4 * ticks - 8 : 4 * ticks - 4]
    operands = weights + (cols, hid, s1, s2, pt, pr, ps, pe)
    parts = (chips, rank, piece)
    extra = [(parts, F32), (parts, BF16)] if fast else [((rank, total), F32)]
    up, gb, ga, leaving, *factor = call(
        functools.partial(last_body, side, ticks - 1),
        "last_tick",
        (x, arrived, loss) + operands,
        [(image, BF16)] + grads + extra,
        (padded, tap_space, pltpu.VMEM((rank, total), F32)),
    )
    operands = (mr, ms, me, cols, hid, up, gb, ga)
    matrices = call(
        functools.partial(finish_body, ticks - 1),
        "final_sums",
        (x,) + operands,
        [((mid, out), BF16), ((mid, taps), BF16), ((mid, out), BF16)],
    )
    if not fast:
        bases, rights = general_tail(factor[0], matrices, splits)
        return tuple(value[None] for value in [leaving[None], *bases, *rights])

    def scattered(keep, send, name):
        got = swap(send, flips(0, True))
        own, *sends = call(
            fold_body,
            name,
            (keep, got),
            [(keep.shape[1:], F32)] + [(keep.shape[1:], BF16)] * (chips - 1),
        )
        return own, [swap(value, flips(chip, False)) for chip, value in enumerate(sends, 1)]

    own, others = scattered(*factor, "fold_factor")
    (own,) = call(
        total_body,
        "total_factor",
        (own, *others),
        [((rank, piece), BF16)],
    )
    mine = [own] + [swap(own, flips(chip, False)) for chip in range(1, chips)]
    other = swap(jnp.stack(mine), flips(0, True))
    part = (mid + mid + out) // replicas
    operands = (*mine, other, *matrices)
    pt, keep, send = call(
        functools.partial(right_body, chips),
        "right_products",
        operands,
        [((rank, total), BF16), ((chips, rank, part), F32), ((chips, rank, part), BF16)],
        (pltpu.VMEM((rank, total), F32), pltpu.VMEM((replicas, rank, part), F32)),
    )
    own, others = scattered(keep, send, "fold_right")
    inverse, *bases = call(
        functools.partial(basis_body, splits),
        "basis",
        (pt,),
        [((3, rank, rank), F32)] + [((rank, rows // replicas), F32) for rows in splits],
    )
    operands = (inverse, own, *others)
    rights = call(
        functools.partial(end_body, splits, replicas),
        "right_factors",
        operands,
        [((rank, columns // replicas), F32) for columns in (mid, mid, out)],
    )
    return tuple(value[None] for value in [leaving[None], *bases, *rights])


def solution(mesh):
    replica = P("section", REPLICA_AXES)
    weight = P("section")
    column = P("section", None, REPLICA_AXES)
    return jax.shard_map(
        local,
        mesh=mesh,
        in_specs=(replica, replica, P(REPLICA_AXES)) + (weight,) * 3 + (replica,) * 3 + (weight,) * 3,
        out_specs=(replica,) + (column,) * 6,
        check_vma=False,
    )
```

```python
import functools
import math

import jax
import jax.numpy as jnp
from jax import lax
from jax.experimental import pallas as pl
from jax.experimental.pallas import tpu as pltpu
from jax.sharding import PartitionSpec as P


F32 = jnp.float32
BF16 = jnp.bfloat16
PAD = 16
VMEM_LIMIT = 16 * 1024 * 1024
REPLICA_AXES = ("node", "local")
precise = lax.Precision.HIGHEST

NN = (((1,), (0,)), ((), ()))
NT = (((1,), (1,)), ((), ()))
TN = (((0,), (0,)), ((), ()))


def mm(left, right, dims=NN, accuracy=None):
    return lax.dot_general(left, right, dims, precision=accuracy, preferred_element_type=F32)


def call(body, operands, outs, scratch=(), given=0, results=0):
    kept = len(outs) - results
    vmem, hbm = pl.BlockSpec(memory_space=pltpu.VMEM), pl.BlockSpec(memory_space=pltpu.HBM)
    place = pltpu.with_memory_space_constraint
    operands = [place(value, pltpu.HBM) for value in operands[:given]] + [
        place(value, pltpu.VMEM) for value in operands[given:]
    ]
    return pl.pallas_call(
        body,
        in_specs=[hbm] * given + [vmem] * (len(operands) - given),
        out_specs=[vmem] * kept + [hbm] * results,
        out_shape=[pltpu.VMEM(*out) for out in outs[:kept]]
        + [pltpu.HBM(*out) for out in outs[kept:]],
        scratch_shapes=list(scratch),
        compiler_params=pltpu.CompilerParams(vmem_limit_bytes=VMEM_LIMIT),
    )(*operands)


def split(values):
    high = values.astype(BF16)
    low = (values - high.astype(F32)).astype(BF16)
    return jnp.concatenate([high, low], axis=0)


def joined(values):
    rank = values.shape[0] // 2
    return values[:rank] + values[rank:]


def low_rank(prior, grads, inputs):
    inner = joined(mm(split(prior), grads, NT))
    return joined(mm(split(inner), inputs))


def spread_taps(values, padded, columns, side, reverse):
    pixels, channels = values.shape
    column = lax.rem(lax.broadcasted_iota(jnp.int32, (pixels, 1), 0), side)
    zeros = jnp.zeros((PAD, channels), F32)
    for variant in range(3):
        padded[variant, 0:PAD] = zeros
        padded[variant, PAD + pixels : PAD + pixels + PAD] = zeros
    padded[0, PAD : PAD + pixels] = jnp.where(column != side - 1, values, 0.0)
    padded[1, PAD : PAD + pixels] = values
    padded[2, PAD : PAD + pixels] = jnp.where(column != 0, values, 0.0)
    for tap in range(9):
        source = 8 - tap if reverse else tap
        start = PAD + (source // 3 - 1) * side + source % 3 - 1
        columns[:, tap * channels : (tap + 1) * channels] = padded[
            source % 3, start : start + pixels
        ].astype(BF16)


def forward(inputs, w_reduce, w_spatial, padded, columns, hidden, slope_one, slope_two, side):
    pre = mm(inputs[...], w_reduce[...])
    logistic = jax.nn.sigmoid(pre)
    slope_one[...] = logistic * (1.0 + pre * (1.0 - logistic))
    spread_taps(pre * logistic, padded, columns, side, False)
    pre = mm(columns[...], w_spatial[...])
    logistic = jax.nn.sigmoid(pre)
    slope_two[...] = logistic * (1.0 + pre * (1.0 - logistic))
    hidden[...] = (pre * logistic).astype(BF16)


def backward(up, w_reduce, w_spatial, w_expand, slope_one, slope_two, padded, taps, side):
    channels = slope_one.shape[1]
    grad = mm(up, w_expand[...], NT) * slope_two[...]
    spread_taps(grad, padded, taps, side, True)
    back = None
    for tap in range(9):
        block = slice(tap * channels, (tap + 1) * channels)
        term = mm(taps[:, block], w_spatial[block, :], NT)
        back = term if back is None else back + term
    grad_two = grad.astype(BF16)
    grad_one = (back * slope_one[...]).astype(BF16)
    leaving = (up.astype(F32) + mm(grad_one, w_reduce[...], NT)).astype(BF16)
    return grad_two, grad_one, leaving


def first_body(side, x_in, wr_in, ws_in, we_in, up_in, x, wr, ws, we, up, cols, hid, gb, ga, dx,
               raw, padded, taps, s1, s2, sems):
    pairs = ((x_in, raw), (wr_in, wr), (ws_in, ws), (we_in, we), (up_in, up))
    copies = [pltpu.make_async_copy(a, b, sems.at[i]) for i, (a, b) in enumerate(pairs)]
    for copy in copies:
        copy.start()
    copies[0].wait()
    x[...] = jnp.swapaxes(raw[...], 0, 1)
    copies[1].wait()
    copies[2].wait()
    forward(x.at[0], wr, ws, padded, cols, hid, s1, s2, side)
    copies[3].wait()
    copies[4].wait()
    gb[...], ga[...], dx[...] = backward(up[...], wr, ws, we, s1, s2, padded, taps, side)


def ahead_body(side, count, x, wr, ws, *refs):
    padded = refs[-1]
    for step in range(count):
        cols, hid, s1, s2 = refs[4 * step : 4 * step + 4]
        forward(x.at[step + 1], wr, ws, padded, cols, hid, s1, s2, side)


def chosen(arrived, loss, tick):
    last = lax.axis_index("section") == lax.axis_size("section") - 1
    return jnp.where(last, loss[tick - 1], arrived[...])


def middle_body(side, tick, arrived, loss, wr, ws, we, s1, s2, up, gb, ga, dx, padded, taps):
    value = chosen(arrived, loss, tick)
    up[...] = value
    gb[...], ga[...], dx[...] = backward(value, wr, ws, we, s1, s2, padded, taps, side)


def start_body(er, es, ee, pr, ps, pe, pt, etr, ets):
    rows, spatial = er.shape[0], es.shape[0]
    pt[:, 0:rows] = joined(mm(split(pr[...]), er[...], NT))
    pt[:, rows : rows + spatial] = joined(mm(split(ps[...]), es[...], NT))
    pt[:, rows + spatial :] = joined(mm(split(pe[...]), ee[...], NT))
    etr[...] = er[...].astype(F32).T
    ets[...] = es[...].astype(F32).T


def add_factor(pt_in, pt_out, x, cols, hid, up, gb, ga, pr, ps, pe):
    rows, spatial = x.shape[1], cols.shape[1]
    end = rows + spatial
    pt_out[:, 0:rows] = pt_in[:, 0:rows] + low_rank(pr[...], ga, x[...])
    pt_out[:, rows:end] = pt_in[:, rows:end] + low_rank(ps[...], gb, cols[...])
    pt_out[:, end:] = pt_in[:, end:] + low_rank(pe[...], up, hid[...])


def sums_body(count, x, etr, ets, ee, pt, pr, ps, pe, *refs):
    pt_out, mr, ms, me = refs[-4:]
    source = pt
    for step in range(count):
        cols, hid, up, gb, ga = refs[5 * step : 5 * step + 5]
        add_factor(source, pt_out, x.at[step], cols, hid, up[...], gb[...], ga[...], pr, ps, pe)
        source = pt_out
    for step in range(count):
        cols, hid, up, gb, ga = refs[5 * step : 5 * step + 5]
        base_r = etr[...] if step == 0 else mr[...]
        mr[...] = base_r + mm(ga[...], x[step], TN)
        base_s = ets[...] if step == 0 else ms[...]
        ms[...] = base_s + mm(gb[...], cols[...], TN)
        base_e = ee[...].astype(F32) if step == 0 else me[...]
        me[...] = base_e + mm(hid[...], up[...], TN)


def last_body(side, tick, x, arrived, loss, wr, ws, we, cols, hid, s1, s2, pt, pr, ps, pe,
              up, gb, ga, *refs):
    outs, (padded, taps, factor) = refs[:-3], refs[-3:]
    dx = outs[0]
    value = chosen(arrived, loss, tick)
    up[...] = value
    gb[...], ga[...], dx[...] = backward(value, wr, ws, we, s1, s2, padded, taps, side)
    factors = (x.at[tick], cols, hid, value, gb[...], ga[...], pr, ps, pe)
    if len(outs) == 2:
        add_factor(pt, outs[1], *factors)
    else:
        add_factor(pt, factor, *factors)
        keep, send = outs[1:]
        half = keep.shape[1]
        core = core_index()
        keep[...] = factor[:, pl.ds(pl.multiple_of(core * half, 128), half)]
        sent = factor[:, pl.ds(pl.multiple_of((1 - core) * half, 128), half)]
        send[...] = sent.astype(BF16)


def finish_body(tick, x, mr, ms, me, cols, hid, up, gb, ga, br, bs, be):
    br[...] = (mr[...] + mm(ga[...], x[tick], TN)).astype(BF16)
    bs[...] = (ms[...] + mm(gb[...], cols[...], TN)).astype(BF16)
    be[...] = (me[...] + mm(hid[...], up[...], TN)).astype(BF16)


def packed_body(tick, dx, x, mr, ms, me, cols, hid, up, gb, ga, keep, send, leaving,
                tr, ts, te, sem):
    copy = pltpu.make_async_copy(dx, leaving, sem)
    copy.start()
    tr[...] = mr[...] + mm(ga[...], x[tick], TN)
    ts[...] = ms[...] + mm(gb[...], cols[...], TN)
    te[...] = me[...] + mm(hid[...], up[...], TN)
    core = core_index()
    mid, out = tr.shape
    taps = ts.shape[1]
    high, wide = mid // 4, out // 4
    for block in range(2):
        rows = slice(block * high, (block + 1) * high)
        for target, at in ((keep, 2 * block + core), (send, 2 * block + 1 - core)):
            source = pl.ds(pl.multiple_of(at * high, 8), high)
            target[rows, 0:out] = tr[source, :].astype(target.dtype)
            target[rows, out : out + taps] = ts[source, :].astype(target.dtype)
            lanes = pl.ds(pl.multiple_of(at * wide, 128), wide)
            part = te[:, lanes].astype(target.dtype)
            start = out + taps + block * wide
            target[:, start : start + wide] = part[: mid // 2]
            start += 2 * wide
            target[:, start : start + wide] = part[mid // 2 :]
    copy.wait()


def chip_body(keep, got, both):
    both[...] = (keep[...] + got[...].astype(F32)).astype(BF16)


def core_index():
    return lax.rem(lax.axis_index("node"), 2)


def flips(chip, other_core):
    local_bits = lax.axis_size("local").bit_length() - 1
    low = chip & (lax.axis_size("local") - 1)
    high = chip >> local_bits
    return low | (int(other_core) << local_bits) | (high << (local_bits + 1))


def swap(values, mask):
    count = lax.axis_size(REPLICA_AXES)
    return lax.ppermute(values, REPLICA_AXES, [(i, i ^ mask) for i in range(count)])


def total_body(own, flipped_local, flipped_node, flipped_both, total):
    near = own[...].astype(F32) + flipped_local[...].astype(F32)
    far = flipped_node[...].astype(F32) + flipped_both[...].astype(F32)
    total[...] = (near + far).astype(BF16)


def right_body(splits, mine, other, both, pt, keep, *refs):
    sends, pieces = refs[:-1], refs[-1]
    half = mine.shape[1]
    core = core_index()
    pt[:, pl.ds(pl.multiple_of(core * half, 128), half)] = mine[...]
    pt[:, pl.ds(pl.multiple_of((1 - core) * half, 128), half)] = other[...]
    out, taps, _ = splits
    wide = both.shape[1]
    expand = jnp.concatenate([both[:, wide - out : wide - out // 2], both[:, wide - out // 2 :]], 0)
    parts = (
        mm(pt[:, :out], both[:, :out], NT),
        mm(pt[:, out : out + taps], both[:, out : out + taps], NT),
        mm(pt[:, out + taps :], expand),
    )
    count = len(sends) + 1
    for piece in range(count):
        cut = []
        for part in parts:
            size = part.shape[1] // count
            cut.append(part[:, piece * size : (piece + 1) * size])
        pieces[piece] = jnp.concatenate(cut, axis=1)
    local_size = lax.axis_size("local")
    me = lax.axis_index("node") // 2 * local_size + lax.axis_index("local")
    keep[...] = pieces[me]
    for chip, send in enumerate(sends, 1):
        send[...] = pieces[me ^ chip].astype(BF16)


def inverse_factors(grams):
    rank = grams[0].shape[0]
    high = 8
    row = lax.broadcasted_iota(jnp.int32, (high, 1), 0)
    lane = lax.broadcasted_iota(jnp.int32, (high, 2 * rank), 1)
    tables, pivots = [], []
    for gram in grams:
        wide = jnp.concatenate([gram, gram], axis=1)
        blocks = []
        for start in range(0, rank, high):
            unit = jnp.where(lane == row + (start + rank), 1.0, 0.0)
            blocks.append(jnp.where(lane < rank, wide[start : start + high], unit))
        tables.append(blocks)
        pivots.append([jnp.ones((high, 1), F32) for _ in blocks])
    for step in range(rank):
        first, at = step // high, step % high
        for blocks, kept in zip(tables, pivots):
            pivot = blocks[first][at : at + 1, step : step + 1]
            line = blocks[first][at : at + 1, :] * (1.0 / pivot)
            kept[first] = jnp.where(row == at, pivot, kept[first])
            for index in range(first, len(blocks)):
                column = blocks[index][:, step : step + 1]
                if index == first:
                    column = jnp.where(row > at, column, 0.0)
                blocks[index] = blocks[index] - column * line
    return [
        jnp.concatenate([block[:, rank:] * lax.rsqrt(p) for block, p in zip(blocks, kept)], 0)
        for blocks, kept in zip(tables, pivots)
    ]


def basis_body(splits, pt, inverse, *refs):
    count = len(splits)
    outs, scratch, sems = refs[:count], refs[count : 2 * count], refs[2 * count]
    me = lax.axis_index(REPLICA_AXES)
    replicas = lax.axis_size(REPLICA_AXES)
    starts = [sum(splits[:member]) for member in range(count)]
    fulls = [pt[:, start : start + rows] for start, rows in zip(starts, splits)]
    linvs = inverse_factors([mm(full, full, NT) for full in fulls])
    copies = []
    for member, (start, rows) in enumerate(zip(starts, splits)):
        inverse[member] = linvs[member]
        wide = rows // replicas
        window = min(-(-wide // 128) * 128 + (128 if 128 % wide and wide % 128 else 0), rows)
        first = me * wide
        aligned = pl.multiple_of(first // 128 * 128, 128)
        block = pt[:, pl.ds(start + aligned, window)].astype(F32)
        moved = pltpu.roll(block, lax.rem(window - (first - aligned), window), 1)
        scratch[member][...] = math.sqrt(rows) * mm(linvs[member], moved[:, :wide], NN, precise)
        copies.append(pltpu.make_async_copy(scratch[member], outs[member], sems.at[member]))
        copies[-1].start()
    for copy in copies:
        copy.wait()


def end_body(splits, replicas, inverse, own, a, b, c, *refs):
    count = len(splits)
    outs, scratch, sems = refs[:count], refs[count : 2 * count], refs[2 * count]
    total = own[...] + a[...].astype(F32) + b[...].astype(F32) + c[...].astype(F32)
    start = 0
    copies = []
    for member in range(count):
        wide = scratch[member].shape[1]
        scale = 1.0 / (replicas * math.sqrt(splits[member]))
        part = total[:, start : start + wide]
        scratch[member][...] = scale * mm(inverse[member], part, NN, precise)
        start += wide
        copies.append(pltpu.make_async_copy(scratch[member], outs[member], sems.at[member]))
        copies[-1].start()
    for copy in copies:
        copy.wait()


def shifted(block):
    count = lax.axis_size("section")
    return lax.ppermute(block, "section", [(i, i - 1) for i in range(1, count)])


def general_tail(pt, matrices, splits):
    replicas = lax.axis_size(REPLICA_AXES)
    me = lax.axis_index(REPLICA_AXES)
    total = lax.psum(pt, REPLICA_AXES)
    bases, rights = [], []
    start = 0
    for member, rows in enumerate(splits):
        part = total[:, start : start + rows]
        start += rows
        triangle = jnp.linalg.cholesky(mm(part, part, NT, precise))
        unit = lax.linalg.triangular_solve(triangle, part, left_side=True, lower=True)
        wide = rows // replicas
        own = lax.dynamic_slice_in_dim(unit, me * wide, wide, 1)
        bases.append(math.sqrt(rows) * own)
        matrix = matrices[member].astype(F32)
        dims = NN if member == 2 else NT
        right = mm(unit, matrix, dims, precise)
        right = lax.psum_scatter(
            right.astype(BF16), REPLICA_AXES, scatter_dimension=1, tiled=True
        ).astype(F32)
        rights.append(right / (replicas * math.sqrt(rows)))
    return bases, rights


def local(
    section_inputs,
    grad_in,
    loss_grad,
    w_reduce,
    w_spatial,
    w_expand,
    err_reduce,
    err_spatial,
    err_expand,
    prior_reduce,
    prior_spatial,
    prior_expand,
):
    x = section_inputs[0, 0]
    loss = loss_grad[0]
    wr, ws, we = w_reduce[0], w_spatial[0], w_expand[0]
    er, es, ee = err_reduce[0, 0], err_spatial[0, 0], err_expand[0, 0]
    pr, ps, pe = prior_reduce[0], prior_spatial[0], prior_expand[0]
    ticks, pixels, out = x.shape
    mid = wr.shape[1]
    taps = ws.shape[0]
    rank = pr.shape[0]
    side = math.isqrt(pixels)
    total = out + taps + mid
    splits = (out, taps, mid)

    image = (pixels, out)
    inner = (pixels, mid)
    wide = (pixels, taps)
    padded = pltpu.VMEM((3, pixels + 2 * PAD, mid), F32)
    tap_space = pltpu.VMEM(wide, BF16)
    saved = [(wide, BF16), (inner, BF16), (inner, F32), (inner, F32)]
    grads = [(inner, BF16), (inner, BF16), (image, BF16)]

    matrices = [(wr.shape, BF16), (ws.shape, BF16), (we.shape, BF16)]
    x, wr, ws, we, up, cols, hid, gb, ga, dx = call(
        functools.partial(first_body, side),
        (jnp.swapaxes(x, 0, 1), wr, ws, we, grad_in[0, 0]),
        [(x.shape, BF16)] + matrices + [(image, BF16)] + saved[:2] + grads,
        (
            pltpu.VMEM((pixels, ticks, out), BF16),
            padded,
            tap_space,
            pltpu.VMEM(inner, F32),
            pltpu.VMEM(inner, F32),
            pltpu.SemaphoreType.DMA((5,)),
        ),
        given=5,
    )
    weights = (wr, ws, we)
    done = [(cols, hid, up, gb, ga)]
    arrived = shifted(dx)
    ahead = call(
        functools.partial(ahead_body, side, ticks - 1), (x, wr, ws), saved * (ticks - 1), (padded,)
    )
    pt, etr, ets = call(
        start_body,
        (er, es, ee, pr, ps, pe),
        [((rank, total), F32), ((mid, out), F32), ((mid, taps), F32)],
    )
    for tick in range(1, ticks - 1):
        cols, hid, s1, s2 = ahead[4 * tick - 4 : 4 * tick]
        operands = weights + (s1, s2)
        up, gb, ga, dx = call(
            functools.partial(middle_body, side, tick),
            (arrived, loss) + operands,
            [(image, BF16)] + grads,
            (padded, tap_space),
        )
        done.append((cols, hid, up, gb, ga))
        arrived = shifted(dx)
    flat = tuple(part for group in done for part in group)
    operands = (x, etr, ets, ee, pt, pr, ps, pe) + flat
    pt, mr, ms, me = call(
        functools.partial(sums_body, ticks - 1),
        operands,
        [((rank, total), F32), ((mid, out), F32), ((mid, taps), F32), ((mid, out), F32)],
    )

    replicas = lax.axis_size(REPLICA_AXES)
    fast = lax.axis_size("node") == 4 and lax.axis_size("local") == 2 and total % 256 == 0
    chips = replicas // 2
    half = total // 2
    cols, hid, s1, s2 = ahead[4 * ticks - 8 : 4 * ticks - 4]
    extra = [((rank, half), F32), ((rank, half), BF16)] if fast else [((rank, total), F32)]
    up, gb, ga, leaving, *factor = call(
        functools.partial(last_body, side, ticks - 1),
        (x, arrived, loss) + weights + (cols, hid, s1, s2, pt, pr, ps, pe),
        [(image, BF16)] + grads + extra,
        (padded, tap_space, pltpu.VMEM((rank, total), F32)),
    )
    sums = (x, mr, ms, me, cols, hid, up, gb, ga)
    if not fast:
        matrices = call(
            functools.partial(finish_body, ticks - 1),
            sums,
            [((mid, out), BF16), ((mid, taps), BF16), ((mid, out), BF16)],
        )
        bases, rights = general_tail(factor[0], matrices, splits)
        return tuple(value[None] for value in [leaving[None], *bases, *rights])

    keep, send = factor
    (own,) = call(chip_body, (keep, swap(send, flips(0, True))), [((rank, half), BF16)])
    others = []
    for chip in range(1, chips):
        others.append(swap(own, flips(chip, False)))
    packed = (mid // 2, out + taps + out)
    keep, send, leaving = call(
        functools.partial(packed_body, ticks - 1),
        (leaving,) + sums,
        [(packed, F32), (packed, BF16), (image, BF16)],
        [pltpu.VMEM((mid, out), F32), pltpu.VMEM((mid, taps), F32), pltpu.VMEM((mid, out), F32)]
        + [pltpu.SemaphoreType.DMA],
        results=1,
    )
    (both,) = call(chip_body, (keep, swap(send, flips(0, True))), [(packed, BF16)])
    (mine,) = call(total_body, (own, *others), [((rank, half), BF16)])
    part = (mid + mid + out) // replicas
    pt, keep, *sends = call(
        functools.partial(right_body, splits),
        (mine, swap(mine, flips(0, True)), both),
        [((rank, total), BF16), ((rank, part), F32)] + [((rank, part), BF16)] * (chips - 1),
        [pltpu.VMEM((chips, rank, part), F32)],
    )
    others = [swap(send, flips(chip, False)) for chip, send in enumerate(sends, 1)]
    shapes = [(rank, rows // replicas) for rows in splits]
    inverse, *bases = call(
        functools.partial(basis_body, splits),
        (pt,),
        [((3, rank, rank), F32)] + [(shape, F32) for shape in shapes],
        [pltpu.VMEM(shape, F32) for shape in shapes] + [pltpu.SemaphoreType.DMA((3,))],
        results=3,
    )
    shapes = [(rank, columns // replicas) for columns in (mid, mid, out)]
    rights = call(
        functools.partial(end_body, splits, replicas),
        (inverse, keep, *others),
        [(shape, F32) for shape in shapes],
        [pltpu.VMEM(shape, F32) for shape in shapes] + [pltpu.SemaphoreType.DMA((3,))],
        results=3,
    )
    return tuple(value[None] for value in [leaving[None], *bases, *rights])


def solution(mesh):
    replica = P("section", REPLICA_AXES)
    weight = P("section")
    column = P("section", None, REPLICA_AXES)
    return jax.shard_map(
        local,
        mesh=mesh,
        in_specs=(replica, replica, P(REPLICA_AXES)) + (weight,) * 3 + (replica,) * 3 + (weight,) * 3,
        out_specs=(replica,) + (column,) * 6,
        check_vma=False,
    )
```

```python
import functools
import math

import jax
import jax.numpy as jnp
from jax import lax
from jax.experimental import pallas as pl
from jax.experimental.pallas import tpu as pltpu
from jax.sharding import PartitionSpec as P


F32 = jnp.float32
BF16 = jnp.bfloat16
PAD = 16
VMEM_LIMIT = 16 * 1024 * 1024
REPLICA_AXES = ("node", "local")
precise = lax.Precision.HIGHEST

NN = (((1,), (0,)), ((), ()))
NT = (((1,), (1,)), ((), ()))
TN = (((0,), (0,)), ((), ()))


def mm(left, right, dims=NN, accuracy=None):
    return lax.dot_general(left, right, dims, precision=accuracy, preferred_element_type=F32)


def call(body, operands, outs, scratch=(), given=0, results=0):
    kept = len(outs) - results
    vmem, hbm = pl.BlockSpec(memory_space=pltpu.VMEM), pl.BlockSpec(memory_space=pltpu.HBM)
    place = pltpu.with_memory_space_constraint
    operands = [place(value, pltpu.HBM) for value in operands[:given]] + [
        place(value, pltpu.VMEM) for value in operands[given:]
    ]
    return pl.pallas_call(
        body,
        in_specs=[hbm] * given + [vmem] * (len(operands) - given),
        out_specs=[vmem] * kept + [hbm] * results,
        out_shape=[pltpu.VMEM(*out) for out in outs[:kept]]
        + [pltpu.HBM(*out) for out in outs[kept:]],
        scratch_shapes=list(scratch),
        compiler_params=pltpu.CompilerParams(vmem_limit_bytes=VMEM_LIMIT),
    )(*operands)


def split(values):
    high = values.astype(BF16)
    low = (values - high.astype(F32)).astype(BF16)
    return jnp.concatenate([high, low], axis=0)


def joined(values):
    rank = values.shape[0] // 2
    return values[:rank] + values[rank:]


def low_rank(prior, grads, inputs):
    inner = joined(mm(split(prior), grads, NT))
    return joined(mm(split(inner), inputs))


def spread_taps(values, padded, columns, side, reverse):
    pixels, channels = values.shape
    column = lax.rem(lax.broadcasted_iota(jnp.int32, (pixels, 1), 0), side)
    zeros = jnp.zeros((PAD, channels), F32)
    for variant in range(3):
        padded[variant, 0:PAD] = zeros
        padded[variant, PAD + pixels : PAD + pixels + PAD] = zeros
    padded[0, PAD : PAD + pixels] = jnp.where(column != side - 1, values, 0.0)
    padded[1, PAD : PAD + pixels] = values
    padded[2, PAD : PAD + pixels] = jnp.where(column != 0, values, 0.0)
    for tap in range(9):
        source = 8 - tap if reverse else tap
        start = PAD + (source // 3 - 1) * side + source % 3 - 1
        columns[:, tap * channels : (tap + 1) * channels] = padded[
            source % 3, start : start + pixels
        ].astype(BF16)


def forward(inputs, w_reduce, w_spatial, padded, columns, hidden, slope_one, slope_two, side,
            ready=None):
    pre = mm(inputs[...], w_reduce[...])
    logistic = jax.nn.sigmoid(pre)
    slope_one[...] = logistic * (1.0 + pre * (1.0 - logistic))
    spread_taps(pre * logistic, padded, columns, side, False)
    if ready is not None:
        ready()
    pre = mm(columns[...], w_spatial[...])
    logistic = jax.nn.sigmoid(pre)
    slope_two[...] = logistic * (1.0 + pre * (1.0 - logistic))
    hidden[...] = (pre * logistic).astype(BF16)


def upper(up, w_expand, slope_two):
    return (mm(up, w_expand[...], NT) * slope_two[...]).astype(BF16)


def lower(up, grad_two, w_reduce, w_spatial, slope_one, padded, taps, side):
    channels = slope_one.shape[1]
    spread_taps(grad_two.astype(F32), padded, taps, side, True)
    back = None
    for tap in range(9):
        block = slice(tap * channels, (tap + 1) * channels)
        term = mm(taps[:, block], w_spatial[block, :], NT)
        back = term if back is None else back + term
    grad_one = (back * slope_one[...]).astype(BF16)
    leaving = (up.astype(F32) + mm(grad_one, w_reduce[...], NT)).astype(BF16)
    return grad_one, leaving


def backward(up, w_reduce, w_spatial, w_expand, slope_one, slope_two, padded, taps, side):
    grad_two = upper(up, w_expand, slope_two)
    grad_one, leaving = lower(up, grad_two, w_reduce, w_spatial, slope_one, padded, taps, side)
    return grad_two, grad_one, leaving


def first_body(side, x_in, wr_in, ws_in, we_in, up_in, x, wr, ws, we, up, cols, hid, gb, ga, dx,
               raw, padded, taps, s1, s2, sems):
    pairs = ((x_in, raw), (wr_in, wr), (ws_in, ws), (we_in, we), (up_in, up))
    copies = [pltpu.make_async_copy(a, b, sems.at[i]) for i, (a, b) in enumerate(pairs)]
    for copy in copies:
        copy.start()
    copies[0].wait()
    x[...] = jnp.swapaxes(raw[...], 0, 1)
    copies[1].wait()
    forward(x.at[0], wr, ws, padded, cols, hid, s1, s2, side, copies[2].wait)
    copies[3].wait()
    copies[4].wait()
    gb[...], ga[...], dx[...] = backward(up[...], wr, ws, we, s1, s2, padded, taps, side)


def ahead_body(side, count, x, wr, ws, *refs):
    padded = refs[-1]
    for step in range(count):
        cols, hid, s1, s2 = refs[4 * step : 4 * step + 4]
        forward(x.at[step + 1], wr, ws, padded, cols, hid, s1, s2, side)


def chosen(arrived, loss, tick):
    last = lax.axis_index("section") == lax.axis_size("section") - 1
    return jnp.where(last, loss[tick - 1], arrived[...])


def middle_body(side, tick, arrived, loss, wr, ws, we, s1, s2, up, gb, ga, dx, padded, taps):
    value = chosen(arrived, loss, tick)
    up[...] = value
    gb[...], ga[...], dx[...] = backward(value, wr, ws, we, s1, s2, padded, taps, side)


def start_body(er, es, ee, pr, ps, pe, pt, etr, ets):
    rows, spatial = er.shape[0], es.shape[0]
    pt[:, 0:rows] = joined(mm(split(pr[...]), er[...], NT))
    pt[:, rows : rows + spatial] = joined(mm(split(ps[...]), es[...], NT))
    pt[:, rows + spatial :] = joined(mm(split(pe[...]), ee[...], NT))
    etr[...] = er[...].astype(F32).T
    ets[...] = es[...].astype(F32).T


def add_factor(pt_in, pt_out, x, cols, hid, up, gb, ga, pr, ps, pe):
    rows, spatial = x.shape[1], cols.shape[1]
    end = rows + spatial
    pt_out[:, 0:rows] = pt_in[:, 0:rows] + low_rank(pr[...], ga, x[...])
    pt_out[:, rows:end] = pt_in[:, rows:end] + low_rank(ps[...], gb, cols[...])
    pt_out[:, end:] = pt_in[:, end:] + low_rank(pe[...], up, hid[...])


def sums_body(count, x, etr, ets, ee, pt, pr, ps, pe, *refs):
    pt_out, mr, ms, me = refs[-4:]
    source = pt
    for step in range(count):
        cols, hid, up, gb, ga = refs[5 * step : 5 * step + 5]
        add_factor(source, pt_out, x.at[step], cols, hid, up[...], gb[...], ga[...], pr, ps, pe)
        source = pt_out
    for step in range(count):
        cols, hid, up, gb, ga = refs[5 * step : 5 * step + 5]
        base_r = etr[...] if step == 0 else mr[...]
        mr[...] = base_r + mm(ga[...], x[step], TN)
        base_s = ets[...] if step == 0 else ms[...]
        ms[...] = base_s + mm(gb[...], cols[...], TN)
        base_e = ee[...].astype(F32) if step == 0 else me[...]
        me[...] = base_e + mm(hid[...], up[...], TN)


def head_body(tick, arrived, loss, we, cols, hid, s2, pt, ps, pe, up, gb, *refs):
    outs, factor = refs[:-1], refs[-1]
    value = chosen(arrived, loss, tick)
    up[...] = value
    grad = upper(value, we, s2)
    gb[...] = grad
    spatial = cols.shape[1]
    start = pt.shape[1] - factor.shape[1]
    factor[:, :spatial] = pt[:, start : start + spatial] + low_rank(ps[...], grad, cols[...])
    factor[:, spatial:] = pt[:, start + spatial :] + low_rank(pe[...], value, hid[...])
    if len(outs) == 1:
        outs[0][...] = factor[...]
        return
    keep, send = outs
    half = keep.shape[1]
    core = core_index()
    keep[...] = factor[:, pl.ds(pl.multiple_of(core * half, 128), half)]
    sent = factor[:, pl.ds(pl.multiple_of((1 - core) * half, 128), half)]
    send[...] = sent.astype(BF16)


def tail_body(side, tick, x, up, gb, wr, ws, s1, pt, pr, ga, dx, factor, padded, taps):
    grad, dx[...] = lower(up[...], gb[...], wr, ws, s1, padded, taps, side)
    ga[...] = grad
    rows = factor.shape[1]
    total = pt[:, :rows] + low_rank(pr[...], grad, x[tick])
    factor[...] = total.astype(factor.dtype)


def finish_body(tick, x, mr, ms, me, cols, hid, up, gb, ga, br, bs, be):
    br[...] = (mr[...] + mm(ga[...], x[tick], TN)).astype(BF16)
    bs[...] = (ms[...] + mm(gb[...], cols[...], TN)).astype(BF16)
    be[...] = (me[...] + mm(hid[...], up[...], TN)).astype(BF16)


def packed_body(tick, dx, x, mr, ms, me, cols, hid, up, gb, ga, keep, send, leaving,
                tr, ts, te, sem):
    copy = pltpu.make_async_copy(dx, leaving, sem)
    copy.start()
    tr[...] = mr[...] + mm(ga[...], x[tick], TN)
    ts[...] = ms[...] + mm(gb[...], cols[...], TN)
    te[...] = me[...] + mm(hid[...], up[...], TN)
    core = core_index()
    mid, out = tr.shape
    taps = ts.shape[1]
    high, wide = mid // 4, out // 4
    for block in range(2):
        rows = slice(block * high, (block + 1) * high)
        for target, at in ((keep, 2 * block + core), (send, 2 * block + 1 - core)):
            source = pl.ds(pl.multiple_of(at * high, 8), high)
            target[rows, 0:out] = tr[source, :].astype(target.dtype)
            target[rows, out : out + taps] = ts[source, :].astype(target.dtype)
            lanes = pl.ds(pl.multiple_of(at * wide, 128), wide)
            part = te[:, lanes].astype(target.dtype)
            start = out + taps + block * wide
            target[:, start : start + wide] = part[: mid // 2]
            start += 2 * wide
            target[:, start : start + wide] = part[mid // 2 :]
    copy.wait()


def chip_body(keep, got, both):
    both[...] = (keep[...] + got[...].astype(F32)).astype(BF16)


def gather_body(keep, got, alone, own):
    half = keep.shape[1]
    own[:, :half] = (keep[...] + got[...].astype(F32)).astype(BF16)
    own[:, half:] = alone[...]


def core_index():
    return lax.rem(lax.axis_index("node"), 2)


def flips(chip, other_core):
    local_bits = lax.axis_size("local").bit_length() - 1
    low = chip & (lax.axis_size("local") - 1)
    high = chip >> local_bits
    return low | (int(other_core) << local_bits) | (high << (local_bits + 1))


def swap(values, mask):
    count = lax.axis_size(REPLICA_AXES)
    return lax.ppermute(values, REPLICA_AXES, [(i, i ^ mask) for i in range(count)])


def total_body(own, flipped_local, flipped_node, flipped_both, total):
    near = own[...].astype(F32) + flipped_local[...].astype(F32)
    far = flipped_node[...].astype(F32) + flipped_both[...].astype(F32)
    total[...] = (near + far).astype(BF16)


def right_body(splits, mine, other, both, pt, keep, *refs):
    sends, pieces = refs[:-1], refs[-1]
    out, taps, _ = splits
    half = mine.shape[1] - out
    core = core_index()
    alone = mine[:, half:].astype(F32) + other[:, half:].astype(F32)
    pt[:, :out] = alone.astype(BF16)
    pt[:, pl.ds(pl.multiple_of(out + core * half, 128), half)] = mine[:, :half]
    pt[:, pl.ds(pl.multiple_of(out + (1 - core) * half, 128), half)] = other[:, :half]
    wide = both.shape[1]
    expand = jnp.concatenate([both[:, wide - out : wide - out // 2], both[:, wide - out // 2 :]], 0)
    parts = (
        mm(pt[:, :out], both[:, :out], NT),
        mm(pt[:, out : out + taps], both[:, out : out + taps], NT),
        mm(pt[:, out + taps :], expand),
    )
    count = len(sends) + 1
    for piece in range(count):
        cut = []
        for part in parts:
            size = part.shape[1] // count
            cut.append(part[:, piece * size : (piece + 1) * size])
        pieces[piece] = jnp.concatenate(cut, axis=1)
    local_size = lax.axis_size("local")
    me = lax.axis_index("node") // 2 * local_size + lax.axis_index("local")
    keep[...] = pieces[me]
    for chip, send in enumerate(sends, 1):
        send[...] = pieces[me ^ chip].astype(BF16)


def inverse_factors(grams, width=4):
    rank, high = grams[0].shape[0], 8
    row = lax.broadcasted_iota(jnp.int32, (high, 2 * rank), 0)
    lane = lax.broadcasted_iota(jnp.int32, (high, 2 * rank), 1)
    tables, pivots = [], []
    for gram in grams:
        wide = jnp.concatenate([gram, gram], axis=1)
        blocks = []
        for start in range(0, rank, high):
            unit = jnp.where(lane == row + (start + rank), 1.0, 0.0)
            blocks.append(jnp.where(lane < rank, wide[start : start + high], unit))
        tables.append(blocks)
        pivots.append([jnp.ones((high, 2 * rank), F32) for _ in blocks])
    for step in range(0, rank, width):
        first, at = step // high, step % high
        for blocks, kept in zip(tables, pivots):
            lines = [blocks[first][at + p : at + p + 1] for p in range(width)]
            columns = [
                [jnp.broadcast_to(block[:, step + p : step + p + 1], block.shape) for p in range(width)]
                for block in blocks[first:]
            ]
            entry = [[columns[0][q][at + p : at + p + 1] for q in range(p + 1)] for p in range(width)]
            for p in range(width):
                inverse = 1.0 / entry[p][p]
                kept[first] = jnp.where(row == at + p, entry[p][p], kept[first])
                scaled = lines[p] * inverse
                ratios = [entry[q][p] * inverse for q in range(p + 1, width)]
                for q, ratio in enumerate(ratios, p + 1):
                    lines[q] = lines[q] - ratio * lines[p]
                    for t in range(p + 1, q + 1):
                        entry[q][t] = entry[q][t] - ratio * entry[t][p]
                for index, column in enumerate(columns):
                    factor = column[p]
                    for q, ratio in enumerate(ratios, p + 1):
                        column[q] = column[q] - ratio * factor
                    if index == 0:
                        factor = jnp.where(row >= at + width, factor, 0.0)
                    blocks[first + index] = blocks[first + index] - factor * scaled
            for p in range(1, width):
                blocks[first] = jnp.where(row == at + p, lines[p], blocks[first])
    return [
        jnp.concatenate([(block * lax.rsqrt(p))[:, rank:] for block, p in zip(blocks, kept)], 0)
        for blocks, kept in zip(tables, pivots)
    ]


def basis_body(splits, pt, inverse, *refs):
    count = len(splits)
    outs, scratch, sems = refs[:count], refs[count : 2 * count], refs[2 * count]
    me = lax.axis_index(REPLICA_AXES)
    replicas = lax.axis_size(REPLICA_AXES)
    starts = [sum(splits[:member]) for member in range(count)]
    fulls = [pt[:, start : start + rows] for start, rows in zip(starts, splits)]
    linvs = inverse_factors([mm(full, full, NT) for full in fulls])
    copies = []
    for member, (start, rows) in enumerate(zip(starts, splits)):
        inverse[member] = linvs[member]
        wide = rows // replicas
        window = min(-(-wide // 128) * 128 + (128 if 128 % wide and wide % 128 else 0), rows)
        first = me * wide
        aligned = pl.multiple_of(first // 128 * 128, 128)
        block = pt[:, pl.ds(start + aligned, window)].astype(F32)
        moved = pltpu.roll(block, lax.rem(window - (first - aligned), window), 1)
        scratch[member][...] = math.sqrt(rows) * mm(linvs[member], moved[:, :wide], NN, precise)
        copies.append(pltpu.make_async_copy(scratch[member], outs[member], sems.at[member]))
        copies[-1].start()
    for copy in copies:
        copy.wait()


def end_body(splits, replicas, inverse, own, a, b, c, *refs):
    count = len(splits)
    outs, scratch, sems = refs[:count], refs[count : 2 * count], refs[2 * count]
    total = own[...] + a[...].astype(F32) + b[...].astype(F32) + c[...].astype(F32)
    start = 0
    copies = []
    for member in range(count):
        wide = scratch[member].shape[1]
        scale = 1.0 / (replicas * math.sqrt(splits[member]))
        part = total[:, start : start + wide]
        scratch[member][...] = scale * mm(inverse[member], part, NN, precise)
        start += wide
        copies.append(pltpu.make_async_copy(scratch[member], outs[member], sems.at[member]))
        copies[-1].start()
    for copy in copies:
        copy.wait()


def shifted(block):
    count = lax.axis_size("section")
    return lax.ppermute(block, "section", [(i, i - 1) for i in range(1, count)])


def general_tail(pt, matrices, splits):
    replicas = lax.axis_size(REPLICA_AXES)
    me = lax.axis_index(REPLICA_AXES)
    total = lax.psum(pt, REPLICA_AXES)
    bases, rights = [], []
    start = 0
    for member, rows in enumerate(splits):
        part = total[:, start : start + rows]
        start += rows
        triangle = jnp.linalg.cholesky(mm(part, part, NT, precise))
        unit = lax.linalg.triangular_solve(triangle, part, left_side=True, lower=True)
        wide = rows // replicas
        own = lax.dynamic_slice_in_dim(unit, me * wide, wide, 1)
        bases.append(math.sqrt(rows) * own)
        matrix = matrices[member].astype(F32)
        dims = NN if member == 2 else NT
        right = mm(unit, matrix, dims, precise)
        right = lax.psum_scatter(
            right.astype(BF16), REPLICA_AXES, scatter_dimension=1, tiled=True
        ).astype(F32)
        rights.append(right / (replicas * math.sqrt(rows)))
    return bases, rights


def local(
    section_inputs,
    grad_in,
    loss_grad,
    w_reduce,
    w_spatial,
    w_expand,
    err_reduce,
    err_spatial,
    err_expand,
    prior_reduce,
    prior_spatial,
    prior_expand,
):
    x = section_inputs[0, 0]
    loss = loss_grad[0]
    wr, ws, we = w_reduce[0], w_spatial[0], w_expand[0]
    er, es, ee = err_reduce[0, 0], err_spatial[0, 0], err_expand[0, 0]
    pr, ps, pe = prior_reduce[0], prior_spatial[0], prior_expand[0]
    ticks, pixels, out = x.shape
    mid = wr.shape[1]
    taps = ws.shape[0]
    rank = pr.shape[0]
    side = math.isqrt(pixels)
    total = out + taps + mid
    splits = (out, taps, mid)

    image = (pixels, out)
    inner = (pixels, mid)
    wide = (pixels, taps)
    padded = pltpu.VMEM((3, pixels + 2 * PAD, mid), F32)
    tap_space = pltpu.VMEM(wide, BF16)
    saved = [(wide, BF16), (inner, BF16), (inner, F32), (inner, F32)]
    grads = [(inner, BF16), (inner, BF16), (image, BF16)]

    matrices = [(wr.shape, BF16), (ws.shape, BF16), (we.shape, BF16)]
    x, wr, ws, we, up, cols, hid, gb, ga, dx = call(
        functools.partial(first_body, side),
        (jnp.swapaxes(x, 0, 1), wr, ws, we, grad_in[0, 0]),
        [(x.shape, BF16)] + matrices + [(image, BF16)] + saved[:2] + grads,
        (
            pltpu.VMEM((pixels, ticks, out), BF16),
            padded,
            tap_space,
            pltpu.VMEM(inner, F32),
            pltpu.VMEM(inner, F32),
            pltpu.SemaphoreType.DMA((5,)),
        ),
        given=5,
    )
    weights = (wr, ws, we)
    done = [(cols, hid, up, gb, ga)]
    arrived = shifted(dx)
    ahead = call(
        functools.partial(ahead_body, side, ticks - 1), (x, wr, ws), saved * (ticks - 1), (padded,)
    )
    pt, etr, ets = call(
        start_body,
        (er, es, ee, pr, ps, pe),
        [((rank, total), F32), ((mid, out), F32), ((mid, taps), F32)],
    )
    for tick in range(1, ticks - 1):
        cols, hid, s1, s2 = ahead[4 * tick - 4 : 4 * tick]
        operands = weights + (s1, s2)
        up, gb, ga, dx = call(
            functools.partial(middle_body, side, tick),
            (arrived, loss) + operands,
            [(image, BF16)] + grads,
            (padded, tap_space),
        )
        done.append((cols, hid, up, gb, ga))
        arrived = shifted(dx)
    flat = tuple(part for group in done for part in group)
    operands = (x, etr, ets, ee, pt, pr, ps, pe) + flat
    pt, mr, ms, me = call(
        functools.partial(sums_body, ticks - 1),
        operands,
        [((rank, total), F32), ((mid, out), F32), ((mid, taps), F32), ((mid, out), F32)],
    )

    replicas = lax.axis_size(REPLICA_AXES)
    fast = lax.axis_size("node") == 4 and lax.axis_size("local") == 2 and (taps + mid) % 256 == 0
    chips = replicas // 2
    half = (taps + mid) // 2
    cols, hid, s1, s2 = ahead[4 * ticks - 8 : 4 * ticks - 4]
    extra = [((rank, half), F32), ((rank, half), BF16)] if fast else [((rank, 2 * half), F32)]
    up, gb, *factor = call(
        functools.partial(head_body, ticks - 1),
        (arrived, loss, we, cols, hid, s2, pt, ps, pe),
        [(image, BF16), (inner, BF16)] + extra,
        (pltpu.VMEM((rank, 2 * half), F32),),
    )
    ga, leaving, alone = call(
        functools.partial(tail_body, side, ticks - 1),
        (x, up, gb, wr, ws, s1, pt, pr),
        [(inner, BF16), (image, BF16), ((rank, out), BF16 if fast else F32)],
        (padded, tap_space),
    )
    sums = (x, mr, ms, me, cols, hid, up, gb, ga)
    if not fast:
        matrices = call(
            functools.partial(finish_body, ticks - 1),
            sums,
            [((mid, out), BF16), ((mid, taps), BF16), ((mid, out), BF16)],
        )
        bases, rights = general_tail(jnp.concatenate([alone, factor[0]], 1), matrices, splits)
        return tuple(value[None] for value in [leaving[None], *bases, *rights])

    keep, send = factor
    carried = ((rank, half + out), BF16)
    got = swap(send, flips(0, True))
    (own,) = call(gather_body, (keep, got, alone), [carried])
    others = []
    for chip in range(1, chips):
        others.append(swap(own, flips(chip, False)))
    packed = (mid // 2, out + taps + out)
    keep, send, leaving = call(
        functools.partial(packed_body, ticks - 1),
        (leaving,) + sums,
        [(packed, F32), (packed, BF16), (image, BF16)],
        [pltpu.VMEM((mid, out), F32), pltpu.VMEM((mid, taps), F32), pltpu.VMEM((mid, out), F32)]
        + [pltpu.SemaphoreType.DMA],
        results=1,
    )
    (both,) = call(chip_body, (keep, swap(send, flips(0, True))), [(packed, BF16)])
    (mine,) = call(total_body, (own, *others), [carried])
    part = (mid + mid + out) // replicas
    pt, keep, *sends = call(
        functools.partial(right_body, splits),
        (mine, swap(mine, flips(0, True)), both),
        [((rank, total), BF16), ((rank, part), F32)] + [((rank, part), BF16)] * (chips - 1),
        [pltpu.VMEM((chips, rank, part), F32)],
    )
    others = [swap(send, flips(chip, False)) for chip, send in enumerate(sends, 1)]
    shapes = [(rank, rows // replicas) for rows in splits]
    inverse, *bases = call(
        functools.partial(basis_body, splits),
        (pt,),
        [((3, rank, rank), F32)] + [(shape, F32) for shape in shapes],
        [pltpu.VMEM(shape, F32) for shape in shapes] + [pltpu.SemaphoreType.DMA((3,))],
        results=3,
    )
    shapes = [(rank, columns // replicas) for columns in (mid, mid, out)]
    rights = call(
        functools.partial(end_body, splits, replicas),
        (inverse, keep, *others),
        [(shape, F32) for shape in shapes],
        [pltpu.VMEM(shape, F32) for shape in shapes] + [pltpu.SemaphoreType.DMA((3,))],
        results=3,
    )
    return tuple(value[None] for value in [leaving[None], *bases, *rights])


def solution(mesh):
    replica = P("section", REPLICA_AXES)
    weight = P("section")
    column = P("section", None, REPLICA_AXES)
    return jax.shard_map(
        local,
        mesh=mesh,
        in_specs=(replica, replica, P(REPLICA_AXES)) + (weight,) * 3 + (replica,) * 3 + (weight,) * 3,
        out_specs=(replica,) + (column,) * 6,
        check_vma=False,
    )
```

```python
import functools
import math

import jax
import jax.numpy as jnp
from jax import lax
from jax.experimental import pallas as pl
from jax.experimental.pallas import tpu as pltpu
from jax.sharding import PartitionSpec as P


F32 = jnp.float32
BF16 = jnp.bfloat16
PAD = 16
VMEM_LIMIT = 16 * 1024 * 1024
REPLICA_AXES = ("node", "local")
precise = lax.Precision.HIGHEST

NN = (((1,), (0,)), ((), ()))
NT = (((1,), (1,)), ((), ()))
TN = (((0,), (0,)), ((), ()))


def mm(left, right, dims=NN, accuracy=None):
    return lax.dot_general(left, right, dims, precision=accuracy, preferred_element_type=F32)


def call(body, operands, outs, scratch=(), given=0, results=0):
    kept = len(outs) - results
    vmem, hbm = pl.BlockSpec(memory_space=pltpu.VMEM), pl.BlockSpec(memory_space=pltpu.HBM)
    place = pltpu.with_memory_space_constraint
    operands = [place(value, pltpu.HBM) for value in operands[:given]] + [
        place(value, pltpu.VMEM) for value in operands[given:]
    ]
    return pl.pallas_call(
        body,
        in_specs=[hbm] * given + [vmem] * (len(operands) - given),
        out_specs=[vmem] * kept + [hbm] * results,
        out_shape=[pltpu.VMEM(*out) for out in outs[:kept]]
        + [pltpu.HBM(*out) for out in outs[kept:]],
        scratch_shapes=list(scratch),
        compiler_params=pltpu.CompilerParams(vmem_limit_bytes=VMEM_LIMIT),
    )(*operands)


def split(values):
    high = values.astype(BF16)
    low = (values - high.astype(F32)).astype(BF16)
    return jnp.concatenate([high, low], axis=0)


def joined(values):
    rank = values.shape[0] // 2
    return values[:rank] + values[rank:]


def low_rank(prior, grads, inputs):
    inner = joined(mm(split(prior), grads, NT))
    return joined(mm(split(inner), inputs))


def pad_image(values, padded, side):
    pixels, channels = values.shape
    column = lax.rem(lax.broadcasted_iota(jnp.int32, (pixels, 1), 0), side)
    zeros = jnp.zeros((PAD, channels), F32)
    for variant in range(3):
        padded[variant, 0:PAD] = zeros
        padded[variant, PAD + pixels : PAD + pixels + PAD] = zeros
    padded[0, PAD : PAD + pixels] = jnp.where(column != side - 1, values, 0.0)
    padded[1, PAD : PAD + pixels] = values
    padded[2, PAD : PAD + pixels] = jnp.where(column != 0, values, 0.0)


def shifted_image(padded, tap, side):
    start = PAD + (tap // 3 - 1) * side + tap % 3 - 1
    return padded[tap % 3, start : start + padded.shape[1] - 2 * PAD].astype(BF16)


def forward(inputs, w_reduce, w_spatial, padded, columns, hidden, slope_one, slope_two, side,
            ready=None):
    pre = mm(inputs[...], w_reduce[...])
    logistic = jax.nn.sigmoid(pre)
    slope_one[...] = logistic * (1.0 + pre * (1.0 - logistic))
    pad_image(pre * logistic, padded, side)
    channels = pre.shape[1]
    for tap in range(9):
        columns[:, tap * channels : (tap + 1) * channels] = shifted_image(padded, tap, side)
    if ready is not None:
        ready()
    pre = mm(columns[...], w_spatial[...])
    logistic = jax.nn.sigmoid(pre)
    slope_two[...] = logistic * (1.0 + pre * (1.0 - logistic))
    hidden[...] = (pre * logistic).astype(BF16)


def lower(up, grad_two, w_reduce, w_spatial, slope_one, padded, side, dims):
    channels = slope_one.shape[1]
    pad_image(grad_two.astype(F32), padded, side)
    back = None
    for tap in range(9):
        weight = w_spatial[tap * channels : (tap + 1) * channels, :]
        term = mm(shifted_image(padded, 8 - tap, side), weight, dims)
        back = term if back is None else back + term
    grad_one = (back * slope_one[...]).astype(BF16)
    leaving = (up.astype(F32) + mm(grad_one, w_reduce[...], dims)).astype(BF16)
    return grad_one, leaving


def first_body(side, up_in, we_in, x_in, wr_in, ws_in, up, we, x, wr, ws, cols, hid, gb, ga, dx,
               raw, padded, grad, s1, s2, sems):
    pairs = ((up_in, up), (we_in, we), (x_in, raw), (wr_in, wr), (ws_in, ws))
    copies = [pltpu.make_async_copy(a, b, sems.at[i]) for i, (a, b) in enumerate(pairs)]
    for copy in copies:
        copy.start()
    copies[0].wait()
    copies[1].wait()
    grad[...] = mm(up[...], we[...], NT)
    copies[2].wait()
    x[...] = jnp.swapaxes(raw[...], 0, 1)
    copies[3].wait()
    forward(x.at[0], wr, ws, padded, cols, hid, s1, s2, side, copies[4].wait)
    grad_two = (grad[...] * s2[...]).astype(BF16)
    gb[...] = grad_two
    ga[...], dx[...] = lower(up[...], grad_two, wr, ws, s1, padded, side, NT)


def turn_body(we, wr, ws, we_out, wr_out, ws_out):
    we_out[...] = we[...].astype(F32).T.astype(BF16)
    wr_out[...] = wr[...].astype(F32).T.astype(BF16)
    channels = ws.shape[1]
    for start in range(0, ws.shape[0], channels):
        rows = slice(start, start + channels)
        ws_out[rows, :] = ws[rows, :].astype(F32).T.astype(BF16)


def ahead_body(side, count, x, wr, ws, *refs):
    padded = refs[-1]
    for step in range(count):
        cols, hid, s1, s2 = refs[4 * step : 4 * step + 4]
        forward(x.at[step + 1], wr, ws, padded, cols, hid, s1, s2, side)


def chosen(arrived, loss, tick):
    last = lax.axis_index("section") == lax.axis_size("section") - 1
    return jnp.where(last, loss[tick - 1], arrived[...])


def middle_body(side, tick, arrived, loss, we, wr, ws, s1, s2, up, gb, ga, dx, padded):
    value = chosen(arrived, loss, tick)
    up[...] = value
    grad_two = (mm(value, we[...]) * s2[...]).astype(BF16)
    gb[...] = grad_two
    ga[...], dx[...] = lower(value, grad_two, wr, ws, s1, padded, side, NN)


def start_body(er, es, ee, pr, ps, pe, pt, etr, ets):
    rows, spatial = er.shape[0], es.shape[0]
    pt[:, 0:rows] = joined(mm(split(pr[...]), er[...], NT))
    pt[:, rows : rows + spatial] = joined(mm(split(ps[...]), es[...], NT))
    pt[:, rows + spatial :] = joined(mm(split(pe[...]), ee[...], NT))
    etr[...] = er[...].astype(F32).T
    ets[...] = es[...].astype(F32).T


def add_factor(pt_in, pt_out, x, cols, hid, up, gb, ga, pr, ps, pe):
    rows, spatial = x.shape[1], cols.shape[1]
    end = rows + spatial
    pt_out[:, 0:rows] = pt_in[:, 0:rows] + low_rank(pr[...], ga, x[...])
    pt_out[:, rows:end] = pt_in[:, rows:end] + low_rank(ps[...], gb, cols[...])
    pt_out[:, end:] = pt_in[:, end:] + low_rank(pe[...], up, hid[...])


def sums_body(count, x, etr, ets, ee, pt, pr, ps, pe, *refs):
    pt_out, mr, ms, me = refs[-4:]
    source = pt
    for step in range(count):
        cols, hid, up, gb, ga = refs[5 * step : 5 * step + 5]
        add_factor(source, pt_out, x.at[step], cols, hid, up[...], gb[...], ga[...], pr, ps, pe)
        source = pt_out
    for step in range(count):
        cols, hid, up, gb, ga = refs[5 * step : 5 * step + 5]
        base_r = etr[...] if step == 0 else mr[...]
        mr[...] = base_r + mm(ga[...], x[step], TN)
        base_s = ets[...] if step == 0 else ms[...]
        ms[...] = base_s + mm(gb[...], cols[...], TN)
        base_e = ee[...].astype(F32) if step == 0 else me[...]
        me[...] = base_e + mm(hid[...], up[...], TN)


def head_body(tick, arrived, loss, we, cols, hid, s2, pt, ps, pe, up, gb, *refs):
    outs, factor = refs[:-1], refs[-1]
    value = chosen(arrived, loss, tick)
    up[...] = value
    grad = (mm(value, we[...]) * s2[...]).astype(BF16)
    gb[...] = grad
    spatial = cols.shape[1]
    start = pt.shape[1] - factor.shape[1]
    factor[:, :spatial] = pt[:, start : start + spatial] + low_rank(ps[...], grad, cols[...])
    factor[:, spatial:] = pt[:, start + spatial :] + low_rank(pe[...], value, hid[...])
    if len(outs) == 1:
        outs[0][...] = factor[...]
        return
    keep, send = outs
    half = keep.shape[1]
    core = core_index()
    keep[...] = factor[:, pl.ds(pl.multiple_of(core * half, 128), half)]
    sent = factor[:, pl.ds(pl.multiple_of((1 - core) * half, 128), half)]
    send[...] = sent.astype(BF16)


def tail_body(side, tick, x, up, gb, wr, ws, s1, pt, pr, ga, dx, factor, padded):
    grad, dx[...] = lower(up[...], gb[...], wr, ws, s1, padded, side, NN)
    ga[...] = grad
    rows = factor.shape[1]
    total = pt[:, :rows] + low_rank(pr[...], grad, x[tick])
    factor[...] = total.astype(factor.dtype)


def finish_body(tick, x, mr, ms, me, cols, hid, up, gb, ga, br, bs, be):
    br[...] = (mr[...] + mm(ga[...], x[tick], TN)).astype(BF16)
    bs[...] = (ms[...] + mm(gb[...], cols[...], TN)).astype(BF16)
    be[...] = (me[...] + mm(hid[...], up[...], TN)).astype(BF16)


def packed_body(tick, dx, x, mr, ms, me, cols, hid, up, gb, ga, keep, send, leaving,
                tr, ts, te, sem):
    copy = pltpu.make_async_copy(dx, leaving, sem)
    copy.start()
    tr[...] = mr[...] + mm(ga[...], x[tick], TN)
    ts[...] = ms[...] + mm(gb[...], cols[...], TN)
    te[...] = me[...] + mm(hid[...], up[...], TN)
    core = core_index()
    mid, out = tr.shape
    taps = ts.shape[1]
    high, wide = mid // 4, out // 4
    for block in range(2):
        rows = slice(block * high, (block + 1) * high)
        for target, at in ((keep, 2 * block + core), (send, 2 * block + 1 - core)):
            source = pl.ds(pl.multiple_of(at * high, 8), high)
            target[rows, 0:out] = tr[source, :].astype(target.dtype)
            target[rows, out : out + taps] = ts[source, :].astype(target.dtype)
            lanes = pl.ds(pl.multiple_of(at * wide, 128), wide)
            part = te[:, lanes].astype(target.dtype)
            start = out + taps + block * wide
            target[:, start : start + wide] = part[: mid // 2]
            start += 2 * wide
            target[:, start : start + wide] = part[mid // 2 :]
    copy.wait()


def chip_body(keep, got, both):
    both[...] = (keep[...] + got[...].astype(F32)).astype(BF16)


def gather_body(keep, got, alone, own):
    half = keep.shape[1]
    own[:, :half] = (keep[...] + got[...].astype(F32)).astype(BF16)
    own[:, half:] = alone[...]


def core_index():
    return lax.rem(lax.axis_index("node"), 2)


def flips(chip, other_core):
    local_bits = lax.axis_size("local").bit_length() - 1
    low = chip & (lax.axis_size("local") - 1)
    high = chip >> local_bits
    return low | (int(other_core) << local_bits) | (high << (local_bits + 1))


def swap(values, mask):
    count = lax.axis_size(REPLICA_AXES)
    return lax.ppermute(values, REPLICA_AXES, [(i, i ^ mask) for i in range(count)])


def total_body(own, flipped_local, flipped_node, flipped_both, total):
    near = own[...].astype(F32) + flipped_local[...].astype(F32)
    far = flipped_node[...].astype(F32) + flipped_both[...].astype(F32)
    total[...] = (near + far).astype(BF16)


def right_body(splits, mine, other, both, pt, keep, *refs):
    sends, pieces = refs[:-1], refs[-1]
    out, taps, _ = splits
    half = mine.shape[1] - out
    core = core_index()
    alone = mine[:, half:].astype(F32) + other[:, half:].astype(F32)
    pt[:, :out] = alone.astype(BF16)
    pt[:, pl.ds(pl.multiple_of(out + core * half, 128), half)] = mine[:, :half]
    pt[:, pl.ds(pl.multiple_of(out + (1 - core) * half, 128), half)] = other[:, :half]
    wide = both.shape[1]
    expand = jnp.concatenate([both[:, wide - out : wide - out // 2], both[:, wide - out // 2 :]], 0)
    parts = (
        mm(pt[:, :out], both[:, :out], NT),
        mm(pt[:, out : out + taps], both[:, out : out + taps], NT),
        mm(pt[:, out + taps :], expand),
    )
    count = len(sends) + 1
    for piece in range(count):
        cut = []
        for part in parts:
            size = part.shape[1] // count
            cut.append(part[:, piece * size : (piece + 1) * size])
        pieces[piece] = jnp.concatenate(cut, axis=1)
    local_size = lax.axis_size("local")
    me = lax.axis_index("node") // 2 * local_size + lax.axis_index("local")
    keep[...] = pieces[me]
    for chip, send in enumerate(sends, 1):
        send[...] = pieces[me ^ chip].astype(BF16)


def inverse_factors(grams, width=4):
    rank, high = grams[0].shape[0], 8
    row = lax.broadcasted_iota(jnp.int32, (high, 2 * rank), 0)
    lane = lax.broadcasted_iota(jnp.int32, (high, 2 * rank), 1)
    tables, pivots = [], []
    for gram in grams:
        wide = jnp.concatenate([gram, gram], axis=1)
        blocks = []
        for start in range(0, rank, high):
            unit = jnp.where(lane == row + (start + rank), 1.0, 0.0)
            blocks.append(jnp.where(lane < rank, wide[start : start + high], unit))
        tables.append(blocks)
        pivots.append([jnp.ones((high, 2 * rank), F32) for _ in blocks])
    for step in range(0, rank, width):
        first, at = step // high, step % high
        for blocks, kept in zip(tables, pivots):
            lines = [blocks[first][at + p : at + p + 1] for p in range(width)]
            columns = [
                [jnp.broadcast_to(block[:, step + p : step + p + 1], block.shape) for p in range(width)]
                for block in blocks[first:]
            ]
            entry = [[columns[0][q][at + p : at + p + 1] for q in range(p + 1)] for p in range(width)]
            for p in range(width):
                inverse = 1.0 / entry[p][p]
                kept[first] = jnp.where(row == at + p, entry[p][p], kept[first])
                scaled = lines[p] * inverse
                ratios = [entry[q][p] * inverse for q in range(p + 1, width)]
                for q, ratio in enumerate(ratios, p + 1):
                    lines[q] = lines[q] - ratio * lines[p]
                    for t in range(p + 1, q + 1):
                        entry[q][t] = entry[q][t] - ratio * entry[t][p]
                for index, column in enumerate(columns):
                    factor = column[p]
                    for q, ratio in enumerate(ratios, p + 1):
                        column[q] = column[q] - ratio * factor
                    if index == 0:
                        factor = jnp.where(row >= at + width, factor, 0.0)
                    blocks[first + index] = blocks[first + index] - factor * scaled
            for p in range(1, width):
                blocks[first] = jnp.where(row == at + p, lines[p], blocks[first])
    return [
        jnp.concatenate([(block * lax.rsqrt(p))[:, rank:] for block, p in zip(blocks, kept)], 0)
        for blocks, kept in zip(tables, pivots)
    ]


def basis_body(splits, pt, inverse, *refs):
    count = len(splits)
    outs, scratch, sems = refs[:count], refs[count : 2 * count], refs[2 * count]
    me = lax.axis_index(REPLICA_AXES)
    replicas = lax.axis_size(REPLICA_AXES)
    starts = [sum(splits[:member]) for member in range(count)]
    fulls = [pt[:, start : start + rows] for start, rows in zip(starts, splits)]
    linvs = inverse_factors([mm(full, full, NT) for full in fulls])
    copies = []
    for member, (start, rows) in enumerate(zip(starts, splits)):
        inverse[member] = linvs[member]
        wide = rows // replicas
        window = min(-(-wide // 128) * 128 + (128 if 128 % wide and wide % 128 else 0), rows)
        first = me * wide
        aligned = pl.multiple_of(first // 128 * 128, 128)
        block = pt[:, pl.ds(start + aligned, window)].astype(F32)
        moved = pltpu.roll(block, lax.rem(window - (first - aligned), window), 1)
        scratch[member][...] = math.sqrt(rows) * mm(linvs[member], moved[:, :wide], NN, precise)
        copies.append(pltpu.make_async_copy(scratch[member], outs[member], sems.at[member]))
        copies[-1].start()
    for copy in copies:
        copy.wait()


def end_body(splits, replicas, inverse, own, a, b, c, *refs):
    count = len(splits)
    outs, scratch, sems = refs[:count], refs[count : 2 * count], refs[2 * count]
    total = own[...] + a[...].astype(F32) + b[...].astype(F32) + c[...].astype(F32)
    start = 0
    copies = []
    for member in range(count):
        wide = scratch[member].shape[1]
        scale = 1.0 / (replicas * math.sqrt(splits[member]))
        part = total[:, start : start + wide]
        scratch[member][...] = scale * mm(inverse[member], part, NN, precise)
        start += wide
        copies.append(pltpu.make_async_copy(scratch[member], outs[member], sems.at[member]))
        copies[-1].start()
    for copy in copies:
        copy.wait()


def shifted(block):
    count = lax.axis_size("section")
    return lax.ppermute(block, "section", [(i, i - 1) for i in range(1, count)])


def general_tail(pt, matrices, splits):
    replicas = lax.axis_size(REPLICA_AXES)
    me = lax.axis_index(REPLICA_AXES)
    total = lax.psum(pt, REPLICA_AXES)
    bases, rights = [], []
    start = 0
    for member, rows in enumerate(splits):
        part = total[:, start : start + rows]
        start += rows
        triangle = jnp.linalg.cholesky(mm(part, part, NT, precise))
        unit = lax.linalg.triangular_solve(triangle, part, left_side=True, lower=True)
        wide = rows // replicas
        own = lax.dynamic_slice_in_dim(unit, me * wide, wide, 1)
        bases.append(math.sqrt(rows) * own)
        matrix = matrices[member].astype(F32)
        dims = NN if member == 2 else NT
        right = mm(unit, matrix, dims, precise)
        right = lax.psum_scatter(
            right.astype(BF16), REPLICA_AXES, scatter_dimension=1, tiled=True
        ).astype(F32)
        rights.append(right / (replicas * math.sqrt(rows)))
    return bases, rights


def local(
    section_inputs,
    grad_in,
    loss_grad,
    w_reduce,
    w_spatial,
    w_expand,
    err_reduce,
    err_spatial,
    err_expand,
    prior_reduce,
    prior_spatial,
    prior_expand,
):
    x = section_inputs[0, 0]
    loss = loss_grad[0]
    wr, ws, we = w_reduce[0], w_spatial[0], w_expand[0]
    er, es, ee = err_reduce[0, 0], err_spatial[0, 0], err_expand[0, 0]
    pr, ps, pe = prior_reduce[0], prior_spatial[0], prior_expand[0]
    ticks, pixels, out = x.shape
    mid = wr.shape[1]
    taps = ws.shape[0]
    rank = pr.shape[0]
    side = math.isqrt(pixels)
    total = out + taps + mid
    splits = (out, taps, mid)

    image = (pixels, out)
    inner = (pixels, mid)
    wide = (pixels, taps)
    padded = pltpu.VMEM((3, pixels + 2 * PAD, mid), F32)
    saved = [(wide, BF16), (inner, BF16), (inner, F32), (inner, F32)]
    grads = [(inner, BF16), (inner, BF16), (image, BF16)]

    matrices = [((mid, out), BF16), (x.shape, BF16), ((out, mid), BF16), ((taps, mid), BF16)]
    up, we, x, wr, ws, cols, hid, gb, ga, dx = call(
        functools.partial(first_body, side),
        (grad_in[0, 0], we, jnp.swapaxes(x, 0, 1), wr, ws),
        [(image, BF16)] + matrices + saved[:2] + grads,
        (
            pltpu.VMEM((pixels, ticks, out), BF16),
            padded,
            pltpu.VMEM(inner, F32),
            pltpu.VMEM(inner, F32),
            pltpu.VMEM(inner, F32),
            pltpu.SemaphoreType.DMA((5,)),
        ),
        given=5,
    )
    done = [(cols, hid, up, gb, ga)]
    arrived = shifted(dx)
    turned = call(
        turn_body, (we, wr, ws), [((out, mid), BF16), ((mid, out), BF16), ((taps, mid), BF16)]
    )
    ahead = call(
        functools.partial(ahead_body, side, ticks - 1), (x, wr, ws), saved * (ticks - 1), (padded,)
    )
    pt, etr, ets = call(
        start_body,
        (er, es, ee, pr, ps, pe),
        [((rank, total), F32), ((mid, out), F32), ((mid, taps), F32)],
    )
    for tick in range(1, ticks - 1):
        cols, hid, s1, s2 = ahead[4 * tick - 4 : 4 * tick]
        operands = (*turned, s1, s2)
        up, gb, ga, dx = call(
            functools.partial(middle_body, side, tick),
            (arrived, loss) + operands,
            [(image, BF16)] + grads,
            (padded,),
        )
        done.append((cols, hid, up, gb, ga))
        arrived = shifted(dx)
    flat = tuple(part for group in done for part in group)
    operands = (x, etr, ets, ee, pt, pr, ps, pe) + flat
    pt, mr, ms, me = call(
        functools.partial(sums_body, ticks - 1),
        operands,
        [((rank, total), F32), ((mid, out), F32), ((mid, taps), F32), ((mid, out), F32)],
    )

    replicas = lax.axis_size(REPLICA_AXES)
    fast = lax.axis_size("node") == 4 and lax.axis_size("local") == 2 and (taps + mid) % 256 == 0
    chips = replicas // 2
    half = (taps + mid) // 2
    cols, hid, s1, s2 = ahead[4 * ticks - 8 : 4 * ticks - 4]
    extra = [((rank, half), F32), ((rank, half), BF16)] if fast else [((rank, 2 * half), F32)]
    up, gb, *factor = call(
        functools.partial(head_body, ticks - 1),
        (arrived, loss, turned[0], cols, hid, s2, pt, ps, pe),
        [(image, BF16), (inner, BF16)] + extra,
        (pltpu.VMEM((rank, 2 * half), F32),),
    )
    ga, leaving, alone = call(
        functools.partial(tail_body, side, ticks - 1),
        (x, up, gb, *turned[1:], s1, pt, pr),
        [(inner, BF16), (image, BF16), ((rank, out), BF16 if fast else F32)],
        (padded,),
    )
    sums = (x, mr, ms, me, cols, hid, up, gb, ga)
    if not fast:
        matrices = call(
            functools.partial(finish_body, ticks - 1),
            sums,
            [((mid, out), BF16), ((mid, taps), BF16), ((mid, out), BF16)],
        )
        bases, rights = general_tail(jnp.concatenate([alone, factor[0]], 1), matrices, splits)
        return tuple(value[None] for value in [leaving[None], *bases, *rights])

    keep, send = factor
    carried = ((rank, half + out), BF16)
    got = swap(send, flips(0, True))
    (own,) = call(gather_body, (keep, got, alone), [carried])
    others = []
    for chip in range(1, chips):
        others.append(swap(own, flips(chip, False)))
    packed = (mid // 2, out + taps + out)
    keep, send, leaving = call(
        functools.partial(packed_body, ticks - 1),
        (leaving,) + sums,
        [(packed, F32), (packed, BF16), (image, BF16)],
        [pltpu.VMEM((mid, out), F32), pltpu.VMEM((mid, taps), F32), pltpu.VMEM((mid, out), F32)]
        + [pltpu.SemaphoreType.DMA],
        results=1,
    )
    (both,) = call(chip_body, (keep, swap(send, flips(0, True))), [(packed, BF16)])
    (mine,) = call(total_body, (own, *others), [carried])
    part = (mid + mid + out) // replicas
    pt, keep, *sends = call(
        functools.partial(right_body, splits),
        (mine, swap(mine, flips(0, True)), both),
        [((rank, total), BF16), ((rank, part), F32)] + [((rank, part), BF16)] * (chips - 1),
        [pltpu.VMEM((chips, rank, part), F32)],
    )
    others = []
    for chip, send in enumerate(sends, 1):
        others.append(swap(send, flips(chip, False)))
    shapes = [(rank, rows // replicas) for rows in splits]
    inverse, *bases = call(
        functools.partial(basis_body, splits),
        (pt,),
        [((3, rank, rank), F32)] + [(shape, F32) for shape in shapes],
        [pltpu.VMEM(shape, F32) for shape in shapes] + [pltpu.SemaphoreType.DMA((3,))],
        results=3,
    )
    shapes = [(rank, columns // replicas) for columns in (mid, mid, out)]
    rights = call(
        functools.partial(end_body, splits, replicas),
        (inverse, keep, *others),
        [(shape, F32) for shape in shapes],
        [pltpu.VMEM(shape, F32) for shape in shapes] + [pltpu.SemaphoreType.DMA((3,))],
        results=3,
    )
    return tuple(value[None] for value in [leaving[None], *bases, *rights])


def solution(mesh):
    replica = P("section", REPLICA_AXES)
    weight = P("section")
    column = P("section", None, REPLICA_AXES)
    return jax.shard_map(
        local,
        mesh=mesh,
        in_specs=(replica, replica, P(REPLICA_AXES)) + (weight,) * 3 + (replica,) * 3 + (weight,) * 3,
        out_specs=(replica,) + (column,) * 6,
        check_vma=False,
    )
```
